256 devices in a mesh: gz: 8 (over x, core), xy: 32 (over y, z).
Axes of the slice: x: 4, y: 4, z: 8, core: 2. Of those that a mesh axis runs over, the one named last changes fastest.
Arguments:
- x_start: float32 [2, 8, 64, 512, 128], P(None, None, 'gz', 'xy'), may hold values from -6 to 6
- rhs: float32 [2, 8, 64, 512, 128], P(None, None, 'gz', 'xy'), may hold values from -20 to 20
- wave_sq: float32 [64, 512, 128], P('gz', 'xy'), may hold values from 0.3 to 1.5
- damping: float32 [64, 512, 128], P('gz', 'xy'), may hold values from 0.05 to 0.6
- front: float32 [2, 8192, 8192], P(None, ('gz', 'xy')), may hold values from -0.0703125 to 0.0703125
- front_order: int32 [8, 32, 32], P('gz', 'xy'), may hold values from 0 to 31, each once within a row
- pair_count: int32 [8, 32, 32], P('gz'), may hold values from 0 to 3, as said below
- sep_cell: int32 [8, 32, 96], P('gz', 'xy'), may hold values from 0 to 14463, as said below
Outputs:
- solution: float32 [2, 8, 64, 512, 128], P(None, None, 'gz', 'xy')
- new_residual: float32 [2, 8, 64, 512, 128], P(None, None, 'gz', 'xy')
The draws below stay inside these ranges and needn't reach their ends.
Inputs may be any that keep to these rules, and one draw needn't show every extreme that they name: pair_count[g, o, t] counts the separator cells of brick (g, t) whose front rows belong to owner (g, o). For each g and o exactly one brick has 3, one has 2, 27 have 1 and all others 0, so they sum to 32; which bricks is drawn anew for each owner. `sep_cell`: the 96 entries of one brick are distinct local cell indices of that brick, each on its lowest z plane (z = 0) or its lowest y plane (y = 0). Each row front_order[g, o] is a permutation.
All inputs are finite; a program needn't handle non-finite values.
Results may differ from the reference program's by a relative error of at most 0.00011.
Values sent between devices are 32-bit elements; how exact they have to be, the bound alone decides.
A program may use at most 64 MiB of HBM per device.

```python
import math
import jax
import jax.numpy as jnp
from jax import lax

R = 8
CAP = 3
CZ = 8
CY = 16
NX = 128
SLABS = 8
TILES = 32
NZ = 64
NY = 512
CELLS = 16384
SLOTS = 96
ROWS_OWN = 32
SEP = 8192


def draw_rhs(key, part):
    depth_pos = jnp.arange(NZ, dtype=jnp.float32)[:, None, None] / NZ
    height_pos = jnp.arange(NY, dtype=jnp.float32)[None, :, None] / NY
    growth = jnp.exp(0.5 * jnp.log(3.0) * (depth_pos + height_pos))
    base = jnp.clip(jax.random.normal(key, (2, R, NZ, NY, NX), jnp.float32), -5.0, 5.0)
    return base * growth


def draw_pair_count(key, part):
    keys = jax.random.split(jax.random.fold_in(key, 11), SLABS * TILES)
    places = jnp.arange(TILES, dtype=jnp.int32)
    ones_mask = ((places >= 2) & (places < ROWS_OWN - 3)).astype(jnp.int32)

    def one_owner(owner_key):
        order = jax.random.permutation(owner_key, TILES)
        counts = jnp.zeros((TILES,), jnp.int32).at[order].set(ones_mask)
        counts = counts.at[order[0]].set(CAP).at[order[1]].set(CAP - 1)
        return counts
    return jax.vmap(one_owner)(keys).reshape(SLABS, TILES, TILES).astype(jnp.int32)


def move_front(values, target, place):
    where_now = jnp.argmax((values == target).astype(jnp.int32)).astype(jnp.int32)
    held = values[place]
    return values.at[where_now].set(held).at[place].set(target)


def plane_cells():
    lower_z = jnp.arange(CY * NX, dtype=jnp.int32)
    rest = jnp.arange((CZ - 1) * NX, dtype=jnp.int32)
    lower_y = (rest // NX + 1) * (CY * NX) + rest % NX
    return jnp.concatenate([lower_z, lower_y]).astype(jnp.int32)


def draw_sep_cell(key, part):
    keys = jax.random.split(jax.random.fold_in(key, 23), SLABS * TILES)
    brick_ids = jnp.arange(SLABS * TILES, dtype=jnp.int32)
    candidates = plane_cells()
    top_cell = (CZ - 1) * CY * NX + NX - 1

    def one_brick(brick_key, brick_id):
        shuffled = jax.random.permutation(brick_key, candidates).astype(jnp.int32)
        forced = move_front(move_front(shuffled, top_cell, 0), 0, 1)
        chosen = jnp.where(brick_id == 0, forced, shuffled)
        return chosen[:SLOTS]
    return jax.vmap(one_brick)(keys, brick_ids).reshape(SLABS, TILES, SLOTS).astype(jnp.int32)


def block_scale(stream_key, dims, pieces, smallest, top_value):
    def one(axis_at, shards_of):
        heights = jax.random.uniform(jax.random.fold_in(jax.random.fold_in(stream_key, 6), axis_at), (shards_of,), jnp.float32, smallest / len(pieces), top_value / len(pieces))
        return jnp.repeat(jnp.exp(heights), dims[axis_at] // shards_of).reshape((-1,) + (1,) * (len(dims) - axis_at - 1))

    factor_of = one(*pieces[0])
    for cut in pieces[1:]:
        factor_of = factor_of * one(*cut)
    return factor_of


def centred(own_key, extent, spread, bound, cuts=(), kind=jnp.bfloat16):
    values = spread * jax.random.normal(own_key, extent, jnp.float32)
    if cuts:
        values = values * block_scale(own_key, extent, cuts, -0.22, 0.18)
    return jnp.clip(values, -bound, bound).astype(kind)


def setup_inputs(seed: int = 0) -> dict:
    streams_of = jax.random.split(jax.random.key(seed), 9)
    return {
        "x_start": centred(streams_of[0], (2, R, NZ, NY, NX), 1.0, 6.0, ((2, 8), (3, 32)), jnp.float32),
        "rhs": draw_rhs(jax.random.fold_in(streams_of[8], 71), 0),
        "wave_sq": jnp.clip(jnp.exp(math.log(1.5) - 1.60943787 * jax.random.uniform(streams_of[2], (NZ, NY, NX), jnp.float32) ** block_scale(streams_of[2], (NZ, NY, NX), ((0, 8), (1, 32)), -0.2, 0.2)), 0.3, 1.5),
        "damping": jnp.clip(0.05 + 0.55 * jax.random.uniform(streams_of[3], (NZ, NY, NX), jnp.float32) ** block_scale(streams_of[3], (NZ, NY, NX), ((0, 8), (1, 32)), -0.2, 0.2), 0.05, 0.6),
        "front": jnp.clip(jax.random.uniform(streams_of[4], (2, SEP, SEP), jnp.float32, -0.0703125, 0.0703125) * block_scale(streams_of[4], (2, SEP, SEP), ((1, 256),), -0.4, 0.0), -0.0703125, 0.0703125),
        "front_order": jax.vmap(lambda own: jax.random.permutation(own, ROWS_OWN))(jax.random.split(streams_of[5], SLABS * TILES)).reshape((SLABS, TILES, ROWS_OWN)).astype(jnp.int32),
        "pair_count": draw_pair_count(jax.random.fold_in(streams_of[8], 71), 0),
        "sep_cell": draw_sep_cell(jax.random.fold_in(streams_of[8], 71), 0),
    }


def apply_operator(padded, wave_sq, damping):
    depth, height, width = wave_sq.shape
    centre = padded[:, :, 1:depth + 1, 1:height + 1, 1:width + 1]
    face_sum = jnp.zeros_like(centre)
    edge_sum = jnp.zeros_like(centre)
    corner_sum = jnp.zeros_like(centre)
    for offset_z in (-1, 0, 1):
        for offset_y in (-1, 0, 1):
            for offset_x in (-1, 0, 1):
                nonzero = abs(offset_z) + abs(offset_y) + abs(offset_x)
                if nonzero == 0:
                    continue
                shifted = padded[:, :, 1 + offset_z:1 + offset_z + depth, 1 + offset_y:1 + offset_y + height, 1 + offset_x:1 + offset_x + width]
                if nonzero == 1:
                    face_sum = face_sum + shifted
                elif nonzero == 2:
                    edge_sum = edge_sum + shifted
                else:
                    corner_sum = corner_sum + shifted
    negative_laplace = (128.0 * centre - 14.0 * face_sum - 3.0 * edge_sum - corner_sum) / 30.0
    real_part = negative_laplace[0] - wave_sq * (centre[0] - damping * centre[1])
    imag_part = negative_laplace[1] - wave_sq * (centre[1] + damping * centre[0])
    return jnp.stack([real_part, imag_part])


def scale_diagonal(field, wave_sq, damping):
    diag_real = 128.0 / 30.0 - wave_sq
    diag_imag = -wave_sq * damping
    modulus = diag_real * diag_real + diag_imag * diag_imag
    return jnp.stack([(field[0] * diag_real + field[1] * diag_imag) / modulus, (field[1] * diag_real - field[0] * diag_imag) / modulus])


def pad_all(field):
    return jnp.pad(field, ((0, 0), (0, 0), (1, 1), (1, 1), (1, 1)))


def to_bricks(field):
    return field.reshape(2, R, SLABS, CZ, TILES, CY, NX).transpose(2, 4, 0, 1, 3, 5, 6).reshape(SLABS, TILES, 2 * R, CELLS)


def from_bricks(bricks):
    return bricks.reshape(SLABS, TILES, 2, R, CZ, CY, NX).transpose(2, 3, 0, 4, 1, 5, 6).reshape(2, R, NZ, NY, NX)


def add_correction(brick_field, brick_cells, brick_extra):
    return brick_field.at[:, brick_cells].add(brick_extra)


def reference(x_start, rhs, wave_sq, damping, front, front_order, pair_count, sep_cell):
    highest = lax.Precision.HIGHEST
    residual = rhs - apply_operator(pad_all(x_start), wave_sq, damping)
    scaled = scale_diagonal(residual, wave_sq, damping)
    bricked = to_bricks(residual)
    slot_vals = jnp.take_along_axis(bricked, sep_cell[:, :, None, :], axis=3)
    slot_ids = jnp.arange(SLOTS, dtype=jnp.int32)
    owner_of = slot_ids // CAP
    rank_in = slot_ids % CAP
    sent = jnp.transpose(pair_count, (0, 2, 1))
    offsets = (jnp.cumsum(pair_count, axis=2) - pair_count).astype(jnp.int32)
    offsets_src = jnp.transpose(offsets, (0, 2, 1))
    count_slot = sent[:, :, owner_of]
    valid_slot = rank_in[None, None, :] < count_slot
    entry = jnp.minimum(offsets_src[:, :, owner_of] + rank_in[None, None, :], ROWS_OWN - 1).astype(jnp.int32)
    slab_ids = jnp.arange(SLABS, dtype=jnp.int32)[:, None, None]
    local_row = front_order[slab_ids, owner_of[None, None, :], entry]
    front_row = ((slab_ids * TILES + owner_of[None, None, :]) * ROWS_OWN + local_row).astype(jnp.int32)
    front_row = jnp.where(valid_slot, front_row, SEP).astype(jnp.int32)
    vectors = jnp.zeros((SEP, 2 * R), jnp.float32).at[front_row.reshape(-1)].set(slot_vals.transpose(0, 1, 3, 2).reshape(-1, 2 * R), mode="drop")
    vec_real = vectors[:, :R]
    vec_imag = vectors[:, R:]
    out_real = jnp.dot(front[0], vec_real, precision=highest, preferred_element_type=jnp.float32) - jnp.dot(front[1], vec_imag, precision=highest, preferred_element_type=jnp.float32)
    out_imag = jnp.dot(front[0], vec_imag, precision=highest, preferred_element_type=jnp.float32) + jnp.dot(front[1], vec_real, precision=highest, preferred_element_type=jnp.float32)
    solved = jnp.concatenate([out_real, out_imag], axis=1)
    returned = solved[jnp.minimum(front_row, SEP - 1)] * valid_slot[..., None].astype(jnp.float32)
    returned = returned.transpose(0, 1, 3, 2)
    corrected = jax.vmap(jax.vmap(add_correction))(to_bricks(scaled), sep_cell, returned)
    direction = from_bricks(corrected)
    image = apply_operator(pad_all(direction), wave_sq, damping)
    num_real = jnp.sum(image[0] * residual[0] + image[1] * residual[1], axis=(1, 2, 3))
    num_imag = jnp.sum(image[0] * residual[1] - image[1] * residual[0], axis=(1, 2, 3))
    denom = jnp.sum(image[0] * image[0] + image[1] * image[1], axis=(1, 2, 3)) + 1e-6
    alpha_real = (num_real / denom)[:, None, None, None]
    alpha_imag = (num_imag / denom)[:, None, None, None]
    solution = jnp.stack([x_start[0] + alpha_real * direction[0] - alpha_imag * direction[1], x_start[1] + alpha_real * direction[1] + alpha_imag * direction[0]])
    new_residual = jnp.stack([residual[0] - alpha_real * image[0] + alpha_imag * image[1], residual[1] - alpha_real * image[1] - alpha_imag * image[0]])
    return (solution, new_residual)
```

```python
import functools

import jax
import jax.numpy as jnp
from jax import lax
from jax.experimental import pallas as pl
from jax.experimental.pallas import tpu as pltpu
from jax.sharding import PartitionSpec as P

MESH = pl.DeviceIdType.MESH
HIGHEST = lax.Precision.HIGHEST
F32 = jnp.float32
BF16 = jnp.bfloat16
LANES = 128


def iota(shape, dim):
    return lax.broadcasted_iota(jnp.int32, shape, dim)


def dot(a, b, contract):
    return lax.dot_general(
        a, b, ((contract[:1], contract[1:]), ((), ())), precision=HIGHEST, preferred_element_type=F32
    )


def x_sum(u):
    axis = u.ndim - 1
    lane = iota(u.shape, axis)
    left = jnp.where(lane > 0, pltpu.roll(u, 1, axis), 0.0)
    right = jnp.where(lane < LANES - 1, pltpu.roll(u, LANES - 1, axis), 0.0)
    return left + right


def side_rows(rows, edge_low, edge_high):
    depth = rows.shape[0]
    row_sum = x_sum(rows)
    m1 = 14.0 * rows + 3.0 * row_sum
    m2 = 3.0 * rows + row_sum
    edge = jnp.where(iota(rows.shape, 0) == 0, edge_low, edge_high)
    m2_edge = 3.0 * edge + x_sum(edge)
    z_pos = iota(rows.shape, 0)
    below = jnp.where(z_pos == 0, m2_edge, pltpu.roll(m2, 1, 0))
    above = jnp.where(z_pos == depth - 1, m2_edge, pltpu.roll(m2, depth - 1, 0))
    return m1 + below + above


def laplace(centre, z_low, z_high, y_low, y_high, edges):
    depth, height, _ = centre.shape
    padded = jnp.concatenate([z_low[None], centre, z_high[None]], axis=0)
    p = x_sum(padded)
    m1 = 14.0 * padded + 3.0 * p
    m2 = 3.0 * padded + p
    same = 128.0 * centre - 14.0 * p[1:-1] - (m1[:-2] + m1[2:])
    side = m1[1:-1] + m2[:-2] + m2[2:]
    low = side_rows(y_low, edges[0], edges[2])
    high = side_rows(y_high, edges[1], edges[3])
    y_pos = iota(centre.shape, 1)
    before = jnp.where(y_pos == 0, low[:, None, :], pltpu.roll(side, 1, 1))
    after = jnp.where(y_pos == height - 1, high[:, None, :], pltpu.roll(side, height - 1, 1))
    return (same - before - after) * (1.0 / 30.0)


def pack_slots(rows, tiles):
    lane = iota((tiles, LANES), 1)
    out = rows[:tiles]
    for k in range(1, 3):
        out = jnp.where(lane < 16 * k, out, pltpu.roll(rows[k * tiles : (k + 1) * tiles], 16 * k, 1))
    return out


def unpack_slots(rows):
    return jnp.concatenate([rows] + [pltpu.roll(rows, LANES - 16 * k, 1) for k in range(1, 3)], axis=0)


def step(
    x_hbm, rhs_hbm, wave_hbm, damp_hbm, front_hbm, order_ref, count_ref, cell_ref,
    sol_ref, new_ref,
    x, rhs, wave, damp, front, split, res, drn, img, coef,
    y_send, e_send, z_got, y_got, e_got,
    slot_send, slot_got, own_send, own_got, vectors, ret_send, ret_got, acc, sum_send, sum_got, sum2_send, sum2_got, alpha,
    load_sem, halo_send_sem, halo_recv_sem, tile_send_sem, tile_recv_sem, slab_send_sem, slab_recv_sem,
):
    slabs, tiles = lax.axis_size("gz"), lax.axis_size("xy")
    g, t = lax.axis_index("gz"), lax.axis_index("xy")
    rhs_count, depth, height = x.shape[1], x.shape[2], x.shape[3]
    comps = 2 * rhs_count
    up_g, down_g = lax.rem(g + 1, slabs), lax.rem(g + slabs - 1, slabs)
    up_t, down_t = lax.rem(t + 1, tiles), lax.rem(t + tiles - 1, tiles)

    loads = [
        pltpu.make_async_copy(src, dst, load_sem.at[i])
        for i, (src, dst) in enumerate(
            [(x_hbm, x), (rhs_hbm, rhs), (wave_hbm, wave), (damp_hbm, damp), (front_hbm, front)]
        )
    ]
    for copy in loads:
        copy.start()

    barrier = pltpu.get_barrier_semaphore()

    def greet(gz, xy):
        pl.semaphore_signal(barrier, inc=1, device_id={"gz": gz, "xy": xy}, device_id_type=MESH)

    def greet_tile(j, carry):
        greet(g, lax.rem(t + j, tiles))
        return carry

    def greet_slab(j, carry):
        greet(lax.rem(g + j, slabs), t)
        return carry

    lax.fori_loop(1, tiles, greet_tile, 0)
    lax.fori_loop(1, slabs, greet_slab, 0)
    for gz in (up_g, down_g):
        for xy in (up_t, down_t):
            greet(gz, xy)

    def remote(src, dst, send_sem, recv_sem, gz, xy):
        return pltpu.make_async_remote_copy(
            src_ref=src, dst_ref=dst, send_sem=send_sem, recv_sem=recv_sem,
            device_id={"gz": gz, "xy": xy}, device_id_type=MESH,
        )

    def pack_halo(field, which):
        low, high = field[:, :, :, 0, :], field[:, :, :, height - 1, :]
        y_send[which, 0] = low
        y_send[which, 1] = high
        e_send[which, 0] = high[:, :, depth - 1, :]
        e_send[which, 1] = low[:, :, depth - 1, :]
        e_send[which, 2] = high[:, :, 0, :]
        e_send[which, 3] = low[:, :, 0, :]

    def halo_copies(field, which):
        todo = [
            (field.at[:, :, depth - 1], z_got.at[which, 0], up_g, t),
            (field.at[:, :, 0], z_got.at[which, 1], down_g, t),
            (y_send.at[which, 1], y_got.at[which, 0], g, up_t),
            (y_send.at[which, 0], y_got.at[which, 1], g, down_t),
            (e_send.at[which, 0], e_got.at[which, 0], up_g, up_t),
            (e_send.at[which, 1], e_got.at[which, 1], up_g, down_t),
            (e_send.at[which, 2], e_got.at[which, 2], down_g, up_t),
            (e_send.at[which, 3], e_got.at[which, 3], down_g, down_t),
        ]
        return [
            remote(src, dst, halo_send_sem.at[which, i], halo_recv_sem.at[which, i], gz, xy)
            for i, (src, dst, gz, xy) in enumerate(todo)
        ]

    has_down_g = (g > 0).astype(F32)
    has_up_g = (g < slabs - 1).astype(F32)
    has_down_t = (t > 0).astype(F32)
    has_up_t = (t < tiles - 1).astype(F32)

    def operator(field, which, r):
        parts = []
        for k in range(2):
            edges = [
                e_got[which, i, k, pl.ds(r, 1), :] * flag
                for i, flag in enumerate(
                    [has_down_g * has_down_t, has_down_g * has_up_t, has_up_g * has_down_t, has_up_g * has_up_t]
                )
            ]
            parts.append(
                laplace(
                    field[k, r],
                    z_got[which, 0, k, r] * has_down_g,
                    z_got[which, 1, k, r] * has_up_g,
                    y_got[which, 0, k, r] * has_down_t,
                    y_got[which, 1, k, r] * has_up_t,
                    edges,
                )
            )
        re, im = field[0, r], field[1, r]
        w, wd = wave[...], damp[...]
        return parts[0] - w * re + wd * im, parts[1] - w * im - wd * re

    def send_rows(send, got, bank):
        def start(j, carry):
            peer = lax.rem(t + j, tiles)
            remote(
                send.at[peer], got.at[t], tile_send_sem.at[bank, peer], tile_recv_sem.at[bank, t], g, peer
            ).start()
            return carry

        lax.fori_loop(1, tiles, start, 0)

    def wait_rows(send, got, bank):
        def wait(j, carry):
            peer = lax.rem(t + j, tiles)
            remote(
                send.at[peer], got.at[peer], tile_send_sem.at[bank, peer], tile_recv_sem.at[bank, peer], g, peer
            ).wait()
            return carry

        lax.fori_loop(1, tiles, wait, 0)

    def spread(send, got, bank):
        def start(j, carry):
            peer = lax.rem(t + j, tiles)
            remote(send, got.at[t], tile_send_sem.at[bank, peer], tile_recv_sem.at[bank, t], g, peer).start()
            return carry

        lax.fori_loop(1, tiles, start, 0)

    def wait_spread(send, got, bank):
        def wait(j, carry):
            peer = lax.rem(t + j, tiles)
            remote(
                send, got.at[peer], tile_send_sem.at[bank, peer], tile_recv_sem.at[bank, peer], g, peer
            ).wait()
            return carry

        lax.fori_loop(1, tiles, wait, 0)

    loads[0].wait()
    pack_halo(x, 0)
    x_halo = halo_copies(x, 0)
    pl.semaphore_wait(barrier, tiles - 1 + slabs - 1 + 4)
    for copy in x_halo:
        copy.start()

    loads[2].wait()
    loads[3].wait()
    w = wave[...]
    wd = w * damp[...]
    damp[...] = wd
    diag_re = 128.0 / 30.0 - w
    diag_im = -wd
    modulus = diag_re * diag_re + diag_im * diag_im
    coef[0] = diag_re / modulus
    coef[1] = diag_im / modulus

    counts = count_ref[0, pl.ds(t, 1), :].astype(F32)
    spread_lane = iota((tiles, LANES), 1)
    spread_row = iota((tiles, LANES), 0)
    rank = spread_lane // tiles
    live = spread_lane < 3 * tiles
    take = jnp.where(live & (spread_row == spread_lane % tiles), 1.0, 0.0)
    earlier = jnp.where(live & (spread_row < spread_lane % tiles), 1.0, 0.0)
    counts8 = jnp.broadcast_to(counts, (8, tiles))
    count_at = dot(counts8, take, (1, 0))[:1]
    entry_at = dot(counts8, earlier, (1, 0))[:1] + rank[:1].astype(F32)
    entry_map = jnp.where((rank.astype(F32) < count_at) & (spread_row.astype(F32) == entry_at), 1.0, 0.0)
    order = order_ref[0, 0:1, :]
    order_map = jnp.where(iota((tiles, tiles), 0) == order, 1.0, 0.0)
    row_map = dot(order_map, entry_map, (1, 0))

    cells = jnp.broadcast_to(cell_ref[0, 0:1, :].astype(F32), (8, cell_ref.shape[2]))
    slots = cell_ref.shape[2]
    slot_row = iota((slots, LANES), 0)
    slot_lane = iota((slots, LANES), 1)
    slot_pick = jnp.where(
        (slot_lane < slots) & (slot_row == 3 * (slot_lane % tiles) + slot_lane // tiles), 1.0, 0.0
    )
    cell_at = (dot(cells, slot_pick, (1, 0))[:1] + 0.5).astype(jnp.int32)
    cell_x = cell_at % LANES
    cell_y = (cell_at // LANES) % height
    cell_z = cell_at // (LANES * height)
    plane_row = jnp.where(cell_z == 0, cell_y, height + cell_z)
    x_map = jnp.where(iota((LANES, LANES), 0) == cell_x, 1.0, 0.0)
    plane_rows = height + depth
    plane_map = jnp.where(iota((plane_rows, LANES), 0) == plane_row, 1.0, 0.0)

    loads[4].wait()
    owned_rows = front.shape[1]
    chunk = 1024

    def split_front(i, carry):
        columns = pl.ds(pl.multiple_of(i * chunk, chunk), chunk)
        for k in range(2):
            value = front[k, :, columns]
            high = value.astype(BF16)
            split[k * owned_rows : (k + 1) * owned_rows, columns] = high
            split[(2 + k) * owned_rows : (3 + k) * owned_rows, columns] = (value - high.astype(F32)).astype(BF16)
        return carry

    lax.fori_loop(0, front.shape[2] // chunk, split_front, 0)

    loads[1].wait()
    for copy in x_halo:
        copy.wait()

    def residual_of(r, carry):
        re, im = operator(x, 0, r)
        re = rhs[0, r] - re
        im = rhs[1, r] - im
        res[0, r] = re
        res[1, r] = im
        drn[0, r] = re * coef[0] + im * coef[1]
        drn[1, r] = im * coef[0] - re * coef[1]
        return carry

    lax.fori_loop(0, rhs_count, residual_of, 0)

    planes = jnp.concatenate(
        [
            res[:, :, 0].reshape(comps, height, LANES),
            res[:, :, :, 0, :].reshape(comps, depth, LANES),
        ],
        axis=1,
    ).reshape(comps * plane_rows, LANES)
    hits = dot(planes, x_map, (1, 0)).reshape(comps, plane_rows, LANES)
    values = jnp.sum(hits * plane_map[None], axis=1)
    values = jnp.concatenate([values, jnp.zeros((LANES - comps, LANES), F32)], axis=0)
    slot_send[:, 0, :] = pack_slots(values.T, tiles)
    send_rows(slot_send, slot_got, 0)
    slot_got[pl.ds(t, 1)] = slot_send[pl.ds(t, 1)]
    wait_rows(slot_send, slot_got, 0)

    by_slot = unpack_slots(slot_got[:, 0, :])
    lane = iota((8, LANES), 1)
    rows4 = jnp.concatenate([row_map[:, : 3 * tiles]] * (LANES // owned_rows), axis=0)
    wide = lax.dot_general(
        by_slot, rows4, (((0,), (1,)), ((), ())), precision=HIGHEST, preferred_element_type=F32
    )
    first, second = wide[:8], wide[8:16]
    block = jnp.where(
        lane < 32, first,
        jnp.where(lane < 64, pltpu.roll(first, 4, 0), jnp.where(lane < 96, second, pltpu.roll(second, 4, 0))),
    )
    own_send[...] = block[:4]
    spread(own_send, own_got, 1)
    own_got[t] = block[:4]
    wait_spread(own_send, own_got, 1)

    groups = tiles // 4
    got = own_got[...].reshape(groups, 4, 4, LANES)
    lane3 = iota((groups, 4, LANES), 2)
    for m in range(4):
        mine = None
        for b in range(4):
            shift = ((b - m) * 32) % LANES
            piece = got[:, b] if shift == 0 else pltpu.roll(got[:, b], shift, 2)
            mine = piece if mine is None else jnp.where(lane3 < 32 * b, mine, piece)
        vectors[pl.ds(g * groups, groups), 4 * m : 4 * m + 4, :] = mine

    def slab_copy(j, src_slab, peer):
        where = pl.ds(src_slab * groups, groups)
        return remote(
            vectors.at[where], vectors.at[where], slab_send_sem.at[0, j], slab_recv_sem.at[0, j], peer, t
        )

    for j in range(1, slabs):
        slab_copy(j, g, lax.rem(g + j, slabs)).start()

    total = jnp.zeros((4 * owned_rows, LANES), F32)
    for j in range(slabs):
        source = lax.rem(g + slabs - j, slabs)
        if j > 0:
            slab_copy(j, source, source).wait_recv()
        vec = jnp.concatenate([vectors[source * groups + a] for a in range(groups)], axis=1)
        high = vec.astype(BF16)
        low = (vec - high.astype(F32)).astype(BF16)
        both = jnp.concatenate([high, low, jnp.zeros((LANES - 2 * comps, vec.shape[1]), BF16)], axis=0)
        width = groups * LANES
        columns = pl.ds(pl.multiple_of(source * width, width), width)
        total = total + lax.dot_general(
            split[:, columns], both, (((1,), (1,)), ((), ())), preferred_element_type=F32
        )
    for j in range(1, slabs):
        slab_copy(j, g, lax.rem(g + j, slabs)).wait_send()
    parts = total[: 2 * owned_rows] + pltpu.roll(total[: 2 * owned_rows], LANES - comps, 1) + total[2 * owned_rows :]
    by_re, by_im = parts[:owned_rows], parts[owned_rows:]
    lane_own = iota((owned_rows, LANES), 1)
    solved = by_re + jnp.where(
        lane_own < rhs_count, -pltpu.roll(by_im, LANES - rhs_count, 1), pltpu.roll(by_im, rhs_count, 1)
    )

    back = lax.dot_general(
        row_map, solved, (((0,), (0,)), ((), ())), precision=HIGHEST, preferred_element_type=F32
    )
    ret_send[:, 0, :] = pack_slots(back, tiles)
    send_rows(ret_send, ret_got, 2)
    ret_got[pl.ds(t, 1)] = ret_send[pl.ds(t, 1)]
    wait_rows(ret_send, ret_got, 2)
    back = unpack_slots(ret_got[:, 0, :])
    back = jnp.concatenate([back, jnp.zeros((LANES - 3 * tiles, LANES), F32)], axis=0)
    values = back.T[:comps]
    placed = (values[:, None, :] * plane_map[None]).reshape(comps * plane_rows, LANES)
    extra = dot(placed, x_map, (1, 1)).reshape(2, rhs_count, plane_rows, LANES)
    drn[:, :, 0] = drn[:, :, 0] + extra[:, :, :height]
    drn[:, :, :, 0, :] = drn[:, :, :, 0, :] + extra[:, :, height:]

    pack_halo(drn, 1)
    d_halo = halo_copies(drn, 1)
    for copy in d_halo:
        copy.start()
    for copy in d_halo:
        copy.wait()

    acc[...] = jnp.zeros_like(acc)

    def image_of(r, carry):
        re, im = operator(drn, 1, r)
        img[0, r] = re
        img[1, r] = im
        res_re, res_im = res[0, r], res[1, r]
        for i, value in enumerate(
            [re * res_re + im * res_im, re * res_im - im * res_re, re * re + im * im]
        ):
            acc[pl.ds(i * rhs_count + r, 1), :] = jnp.sum(jnp.sum(value, axis=0), axis=0, keepdims=True)
        return carry

    lax.fori_loop(0, rhs_count, image_of, 0)

    ones = jnp.ones((8, LANES), F32)
    sum_send[...] = dot(ones, acc[...], (1, 1))[:1]
    spread(sum_send, sum_got, 3)
    sum_got[t] = sum_send[...]
    wait_spread(sum_send, sum_got, 3)
    sum2_send[...] = jnp.sum(sum_got[...], axis=0)

    def sum_copy(j, row, peer):
        return remote(
            sum2_send, sum2_got.at[row], slab_send_sem.at[1, j], slab_recv_sem.at[1, j], peer, t
        )

    for j in range(1, slabs):
        sum_copy(j, g, lax.rem(g + j, slabs)).start()
    sum2_got[g] = sum2_send[...]
    for j in range(1, slabs):
        source = lax.rem(g + slabs - j, slabs)
        sum_copy(j, source, source).wait()
    totals = dot(sum2_got[:, 0, :], jnp.ones((slabs, LANES), F32), (0, 0))
    denom = totals[2 * rhs_count : 3 * rhs_count] + 1e-06
    alpha[0] = totals[:rhs_count] / denom
    alpha[1] = totals[rhs_count : 2 * rhs_count] / denom

    def update(r, carry):
        a_re = alpha[0, pl.ds(r, 1), :][None]
        a_im = alpha[1, pl.ds(r, 1), :][None]
        d_re, d_im = drn[0, r], drn[1, r]
        sol_ref[0, r] = x[0, r] + a_re * d_re - a_im * d_im
        sol_ref[1, r] = x[1, r] + a_re * d_im + a_im * d_re
        i_re, i_im = img[0, r], img[1, r]
        new_ref[0, r] = res[0, r] - a_re * i_re + a_im * i_im
        new_ref[1, r] = res[1, r] - a_re * i_im - a_im * i_re
        return carry

    lax.fori_loop(0, rhs_count, update, 0)


def local(x_start, rhs, wave_sq, damping, front, front_order, pair_count, sep_cell):
    slabs, tiles = lax.axis_size("gz"), lax.axis_size("xy")
    _, rhs_count, depth, height, width = x_start.shape
    field = pltpu.VMEM(x_start.shape, F32)
    any_space = pl.BlockSpec(memory_space=pl.ANY)
    vmem = pl.BlockSpec(memory_space=pltpu.VMEM)
    rows = pltpu.VMEM((tiles, 1, LANES), F32)
    dma = pltpu.SemaphoreType.DMA
    return pl.pallas_call(
        step,
        out_shape=(
            jax.ShapeDtypeStruct(x_start.shape, F32),
            jax.ShapeDtypeStruct(x_start.shape, F32),
        ),
        in_specs=[any_space] * 5 + [vmem] * 3,
        out_specs=(vmem, vmem),
        scratch_shapes=[
            field,
            field,
            pltpu.VMEM(wave_sq.shape, F32),
            pltpu.VMEM(wave_sq.shape, F32),
            pltpu.VMEM(front.shape, F32),
            pltpu.VMEM((4 * front.shape[1], front.shape[2]), BF16),
            field,
            field,
            field,
            pltpu.VMEM((2,) + wave_sq.shape, F32),
            pltpu.VMEM((2, 2, 2, rhs_count, depth, width), F32),
            pltpu.VMEM((2, 4, 2, rhs_count, width), F32),
            pltpu.VMEM((2, 2, 2, rhs_count, height, width), F32),
            pltpu.VMEM((2, 2, 2, rhs_count, depth, width), F32),
            pltpu.VMEM((2, 4, 2, rhs_count, width), F32),
            rows,
            rows,
            pltpu.VMEM((4, LANES), F32),
            pltpu.VMEM((tiles, 4, LANES), F32),
            pltpu.VMEM((slabs * tiles // 4, 2 * rhs_count, LANES), F32),
            rows,
            rows,
            pltpu.VMEM((LANES, LANES), F32),
            pltpu.VMEM((1, LANES), F32),
            rows,
            pltpu.VMEM((1, LANES), F32),
            pltpu.VMEM((slabs, 1, LANES), F32),
            pltpu.VMEM((2, rhs_count, LANES), F32),
            dma((5,)),
            dma((2, 8)),
            dma((2, 8)),
            dma((4, tiles)),
            dma((4, tiles)),
            dma((2, slabs)),
            dma((2, slabs)),
        ],
        compiler_params=pltpu.CompilerParams(
            collective_id=0, has_side_effects=True, vmem_limit_bytes=60 * 1024 * 1024
        ),
    )(x_start, rhs, wave_sq, damping, front, front_order, pair_count, sep_cell)


def solution(mesh):
    in_specs = (
        P(None, None, "gz", "xy", None),
        P(None, None, "gz", "xy", None),
        P("gz", "xy", None),
        P("gz", "xy", None),
        P(None, ("gz", "xy"), None),
        P("gz", "xy", None),
        P("gz", None, None),
        P("gz", "xy", None),
    )
    out_specs = (P(None, None, "gz", "xy", None), P(None, None, "gz", "xy", None))
    return jax.shard_map(local, mesh=mesh, in_specs=in_specs, out_specs=out_specs, check_vma=False)
```

```python
import functools

import jax
import jax.numpy as jnp
from jax import lax
from jax.experimental import pallas as pl
from jax.experimental.pallas import tpu as pltpu
from jax.sharding import PartitionSpec as P

MESH = pl.DeviceIdType.MESH
HIGHEST = lax.Precision.HIGHEST
F32 = jnp.float32
BF16 = jnp.bfloat16
LANES = 128


def iota(shape, dim):
    return lax.broadcasted_iota(jnp.int32, shape, dim)


def dot(a, b, contract):
    return lax.dot_general(
        a, b, ((contract[:1], contract[1:]), ((), ())), precision=HIGHEST, preferred_element_type=F32
    )


def x_sum(u):
    axis = u.ndim - 1
    lane = iota(u.shape, axis)
    left = jnp.where(lane > 0, pltpu.roll(u, 1, axis), 0.0)
    right = jnp.where(lane < LANES - 1, pltpu.roll(u, LANES - 1, axis), 0.0)
    return left + right


def side_rows(rows, edge_low, edge_high):
    depth = rows.shape[0]
    row_sum = x_sum(rows)
    m1 = 14.0 * rows + 3.0 * row_sum
    m2 = 3.0 * rows + row_sum
    edge = jnp.where(iota(rows.shape, 0) == 0, edge_low, edge_high)
    m2_edge = 3.0 * edge + x_sum(edge)
    z_pos = iota(rows.shape, 0)
    below = jnp.where(z_pos == 0, m2_edge, pltpu.roll(m2, 1, 0))
    above = jnp.where(z_pos == depth - 1, m2_edge, pltpu.roll(m2, depth - 1, 0))
    return m1 + below + above


def laplace(centre, z_low, z_high, y_low, y_high, edges):
    depth, height, _ = centre.shape
    padded = jnp.concatenate([z_low[None], centre, z_high[None]], axis=0)
    p = x_sum(padded)
    m1 = 14.0 * padded + 3.0 * p
    m2 = 3.0 * padded + p
    same = 128.0 * centre - 14.0 * p[1:-1] - (m1[:-2] + m1[2:])
    side = m1[1:-1] + m2[:-2] + m2[2:]
    low = side_rows(y_low, edges[0], edges[2])
    high = side_rows(y_high, edges[1], edges[3])
    y_pos = iota(centre.shape, 1)
    before = jnp.where(y_pos == 0, low[:, None, :], pltpu.roll(side, 1, 1))
    after = jnp.where(y_pos == height - 1, high[:, None, :], pltpu.roll(side, height - 1, 1))
    return (same - before - after) * (1.0 / 30.0)


def pack_slots(rows, tiles):
    lane = iota((tiles, LANES), 1)
    out = rows[:tiles]
    for k in range(1, 3):
        out = jnp.where(lane < 16 * k, out, pltpu.roll(rows[k * tiles : (k + 1) * tiles], 16 * k, 1))
    return out


def unpack_slots(rows):
    return jnp.concatenate([rows] + [pltpu.roll(rows, LANES - 16 * k, 1) for k in range(1, 3)], axis=0)


def step(
    x_hbm, rhs_hbm, wave_hbm, damp_hbm, front_hbm, order_hbm, count_hbm, cell_hbm,
    sol_ref, new_ref,
    x, rhs, wave, damp, front, order_ref, count_ref, cell_ref, split, res, drn, img, coef,
    y_send, e_send, z_got, y_got, e_got,
    slot_send, slot_got, own_send, own_got, vectors, ret_send, ret_got, acc, sum_send, sum_got, sum2_send, sum2_got, alpha,
    load_sem, halo_send_sem, halo_recv_sem, tile_send_sem, tile_recv_sem, slab_send_sem, slab_recv_sem,
):
    slabs, tiles = lax.axis_size("gz"), lax.axis_size("xy")
    g, t = lax.axis_index("gz"), lax.axis_index("xy")
    rhs_count, depth, height = x.shape[1], x.shape[2], x.shape[3]
    comps = 2 * rhs_count
    up_g, down_g = lax.rem(g + 1, slabs), lax.rem(g + slabs - 1, slabs)
    up_t, down_t = lax.rem(t + 1, tiles), lax.rem(t + tiles - 1, tiles)

    loads = [
        pltpu.make_async_copy(src, dst, load_sem.at[i])
        for i, (src, dst) in enumerate(
            [
                (x_hbm, x), (rhs_hbm, rhs), (wave_hbm, wave), (damp_hbm, damp), (front_hbm, front),
                (order_hbm, order_ref), (count_hbm, count_ref), (cell_hbm, cell_ref),
            ]
        )
    ]
    loads[0].start()
    barrier = pltpu.get_barrier_semaphore()

    def greet(gz, xy):
        pl.semaphore_signal(barrier, inc=1, device_id={"gz": gz, "xy": xy}, device_id_type=MESH)

    def greet_tile(j, carry):
        greet(g, lax.rem(t + j, tiles))
        return carry

    def greet_slab(j, carry):
        greet(lax.rem(g + j, slabs), t)
        return carry

    lax.fori_loop(1, tiles, greet_tile, 0)
    lax.fori_loop(1, slabs, greet_slab, 0)
    for gz in (up_g, down_g):
        for xy in (up_t, down_t):
            greet(gz, xy)
    for copy in loads[1:]:
        copy.start()

    def remote(src, dst, send_sem, recv_sem, gz, xy):
        return pltpu.make_async_remote_copy(
            src_ref=src, dst_ref=dst, send_sem=send_sem, recv_sem=recv_sem,
            device_id={"gz": gz, "xy": xy}, device_id_type=MESH,
        )

    def pack_halo(field, which):
        low, high = field[:, :, :, 0, :], field[:, :, :, height - 1, :]
        y_send[which, 0] = low
        y_send[which, 1] = high
        e_send[which, 0] = high[:, :, depth - 1, :]
        e_send[which, 1] = low[:, :, depth - 1, :]
        e_send[which, 2] = high[:, :, 0, :]
        e_send[which, 3] = low[:, :, 0, :]

    def halo_copies(field, which):
        todo = [
            (field.at[:, :, depth - 1], z_got.at[which, 0], up_g, t),
            (field.at[:, :, 0], z_got.at[which, 1], down_g, t),
            (y_send.at[which, 1], y_got.at[which, 0], g, up_t),
            (y_send.at[which, 0], y_got.at[which, 1], g, down_t),
            (e_send.at[which, 0], e_got.at[which, 0], up_g, up_t),
            (e_send.at[which, 1], e_got.at[which, 1], up_g, down_t),
            (e_send.at[which, 2], e_got.at[which, 2], down_g, up_t),
            (e_send.at[which, 3], e_got.at[which, 3], down_g, down_t),
        ]
        return [
            remote(src, dst, halo_send_sem.at[which, i], halo_recv_sem.at[which, i], gz, xy)
            for i, (src, dst, gz, xy) in enumerate(todo)
        ]

    has_down_g = (g > 0).astype(F32)
    has_up_g = (g < slabs - 1).astype(F32)
    has_down_t = (t > 0).astype(F32)
    has_up_t = (t < tiles - 1).astype(F32)

    def operator(field, which, r):
        parts = []
        for k in range(2):
            edges = [
                e_got[which, i, k, pl.ds(r, 1), :] * flag
                for i, flag in enumerate(
                    [has_down_g * has_down_t, has_down_g * has_up_t, has_up_g * has_down_t, has_up_g * has_up_t]
                )
            ]
            parts.append(
                laplace(
                    field[k, r],
                    z_got[which, 0, k, r] * has_down_g,
                    z_got[which, 1, k, r] * has_up_g,
                    y_got[which, 0, k, r] * has_down_t,
                    y_got[which, 1, k, r] * has_up_t,
                    edges,
                )
            )
        re, im = field[0, r], field[1, r]
        w, wd = wave[...], damp[...]
        return parts[0] - w * re + wd * im, parts[1] - w * im - wd * re

    def send_rows(send, got, bank):
        def start(j, carry):
            peer = lax.rem(t + j, tiles)
            remote(
                send.at[peer], got.at[t], tile_send_sem.at[bank, peer], tile_recv_sem.at[bank, t], g, peer
            ).start()
            return carry

        lax.fori_loop(1, tiles, start, 0)

    def wait_rows(send, got, bank):
        def wait(j, carry):
            peer = lax.rem(t + j, tiles)
            remote(
                send.at[peer], got.at[peer], tile_send_sem.at[bank, peer], tile_recv_sem.at[bank, peer], g, peer
            ).wait()
            return carry

        lax.fori_loop(1, tiles, wait, 0)

    def spread(send, got, bank):
        def start(j, carry):
            peer = lax.rem(t + j, tiles)
            remote(send, got.at[t], tile_send_sem.at[bank, peer], tile_recv_sem.at[bank, t], g, peer).start()
            return carry

        lax.fori_loop(1, tiles, start, 0)

    def wait_spread(send, got, bank):
        def wait(j, carry):
            peer = lax.rem(t + j, tiles)
            remote(
                send, got.at[peer], tile_send_sem.at[bank, peer], tile_recv_sem.at[bank, peer], g, peer
            ).wait()
            return carry

        lax.fori_loop(1, tiles, wait, 0)

    loads[0].wait()
    pack_halo(x, 0)
    x_halo = halo_copies(x, 0)
    pl.semaphore_wait(barrier, tiles - 1 + slabs - 1 + 4)
    for copy in x_halo[::-1]:
        copy.start()

    loads[2].wait()
    loads[3].wait()
    w = wave[...]
    wd = w * damp[...]
    damp[...] = wd
    diag_re = 128.0 / 30.0 - w
    diag_im = -wd
    modulus = diag_re * diag_re + diag_im * diag_im
    coef[0] = diag_re / modulus
    coef[1] = diag_im / modulus

    for copy in loads[5:]:
        copy.wait()
    counts = count_ref[0, pl.ds(t, 1), :].astype(F32)
    spread_lane = iota((tiles, LANES), 1)
    spread_row = iota((tiles, LANES), 0)
    rank = spread_lane // tiles
    live = spread_lane < 3 * tiles
    take = jnp.where(live & (spread_row == spread_lane % tiles), 1.0, 0.0)
    earlier = jnp.where(live & (spread_row < spread_lane % tiles), 1.0, 0.0)
    counts8 = jnp.broadcast_to(counts, (8, tiles))
    count_at = dot(counts8, take, (1, 0))[:1]
    entry_at = dot(counts8, earlier, (1, 0))[:1] + rank[:1].astype(F32)
    entry_map = jnp.where((rank.astype(F32) < count_at) & (spread_row.astype(F32) == entry_at), 1.0, 0.0)
    order = order_ref[0, 0:1, :]
    order_map = jnp.where(iota((tiles, tiles), 0) == order, 1.0, 0.0)
    row_map = dot(order_map, entry_map, (1, 0))

    cells = jnp.broadcast_to(cell_ref[0, 0:1, :].astype(F32), (8, cell_ref.shape[2]))
    slots = cell_ref.shape[2]
    slot_row = iota((slots, LANES), 0)
    slot_lane = iota((slots, LANES), 1)
    slot_pick = jnp.where(
        (slot_lane < slots) & (slot_row == 3 * (slot_lane % tiles) + slot_lane // tiles), 1.0, 0.0
    )
    cell_at = (dot(cells, slot_pick, (1, 0))[:1] + 0.5).astype(jnp.int32)
    cell_x = cell_at % LANES
    cell_y = (cell_at // LANES) % height
    cell_z = cell_at // (LANES * height)
    plane_row = jnp.where(cell_z == 0, cell_y, height + cell_z)
    x_map = jnp.where(iota((LANES, LANES), 0) == cell_x, 1.0, 0.0)
    plane_rows = height + depth
    plane_map = jnp.where(iota((plane_rows, LANES), 0) == plane_row, 1.0, 0.0)

    loads[4].wait()
    owned_rows = front.shape[1]
    chunk = 1024

    def split_front(i, carry):
        columns = pl.ds(pl.multiple_of(i * chunk, chunk), chunk)
        for k in range(2):
            value = front[k, :, columns]
            high = value.astype(BF16)
            split[k * owned_rows : (k + 1) * owned_rows, columns] = high
            split[(2 + k) * owned_rows : (3 + k) * owned_rows, columns] = (value - high.astype(F32)).astype(BF16)
        return carry

    lax.fori_loop(0, front.shape[2] // chunk, split_front, 0)

    loads[1].wait()
    for copy in x_halo:
        copy.wait()

    def residual_of(r, carry):
        re, im = operator(x, 0, r)
        re = rhs[0, r] - re
        im = rhs[1, r] - im
        res[0, r] = re
        res[1, r] = im
        drn[0, r] = re * coef[0] + im * coef[1]
        drn[1, r] = im * coef[0] - re * coef[1]
        return carry

    lax.fori_loop(0, rhs_count, residual_of, 0)

    planes = jnp.concatenate(
        [
            res[:, :, 0].reshape(comps, height, LANES),
            res[:, :, :, 0, :].reshape(comps, depth, LANES),
        ],
        axis=1,
    ).reshape(comps * plane_rows, LANES)
    hits = dot(planes, x_map, (1, 0)).reshape(comps, plane_rows, LANES)
    values = jnp.sum(hits * plane_map[None], axis=1)
    values = jnp.concatenate([values, jnp.zeros((LANES - comps, LANES), F32)], axis=0)
    slot_send[:, 0, :] = pack_slots(values.T, tiles)
    send_rows(slot_send, slot_got, 0)
    slot_got[pl.ds(t, 1)] = slot_send[pl.ds(t, 1)]
    wait_rows(slot_send, slot_got, 0)

    by_slot = unpack_slots(slot_got[:, 0, :])
    lane = iota((8, LANES), 1)
    rows4 = jnp.concatenate([row_map[:, : 3 * tiles]] * (LANES // owned_rows), axis=0)
    wide = lax.dot_general(
        by_slot, rows4, (((0,), (1,)), ((), ())), precision=HIGHEST, preferred_element_type=F32
    )
    first, second = wide[:8], wide[8:16]
    block = jnp.where(
        lane < 32, first,
        jnp.where(lane < 64, pltpu.roll(first, 4, 0), jnp.where(lane < 96, second, pltpu.roll(second, 4, 0))),
    )
    own_send[...] = block[:4]
    spread(own_send, own_got, 1)
    own_got[t] = block[:4]
    wait_spread(own_send, own_got, 1)

    groups = tiles // 4
    got = own_got[...].reshape(groups, 4, 4, LANES)
    lane3 = iota((groups, 4, LANES), 2)
    for m in range(4):
        mine = None
        for b in range(4):
            shift = ((b - m) * 32) % LANES
            piece = got[:, b] if shift == 0 else pltpu.roll(got[:, b], shift, 2)
            mine = piece if mine is None else jnp.where(lane3 < 32 * b, mine, piece)
        vectors[pl.ds(g * groups, groups), 4 * m : 4 * m + 4, :] = mine

    partner = g + 1 - 2 * lax.rem(g, 2)
    chips = slabs // 2

    def slab_copy(j, source, peer):
        where = pl.ds(source * groups, groups)
        return remote(
            vectors.at[where], vectors.at[where], slab_send_sem.at[0, j], slab_recv_sem.at[0, j], peer, t
        )

    def back_of(base, j):
        return lax.rem(base + slabs - 2 * j, slabs)

    width = groups * LANES

    def product(source):
        vec = jnp.concatenate([vectors[source * groups + a] for a in range(groups)], axis=1)
        high = vec.astype(BF16)
        low = (vec - high.astype(F32)).astype(BF16)
        both = jnp.concatenate([high, low, jnp.zeros((LANES - 2 * comps, vec.shape[1]), BF16)], axis=0)
        columns = pl.ds(pl.multiple_of(source * width, width), width)
        return lax.dot_general(
            split[:, columns], both, (((1,), (1,)), ((), ())), preferred_element_type=F32
        )

    ring = sorted(range(1, chips), key=lambda j: -min(j, chips - j))
    sends = [slab_copy(j, g, lax.rem(g + 2 * j, slabs)) for j in ring] + [slab_copy(chips, g, partner)]
    for copy in sends:
        copy.start()
    total = product(g)
    for j in ring[::-1]:
        slab_copy(j, back_of(g, j), back_of(g, j)).wait_recv()
        onward = slab_copy(chips + j, back_of(g, j), partner)
        onward.start()
        sends.append(onward)
    slab_copy(chips, partner, partner).wait_recv()
    total = total + product(partner)
    for j in ring[::-1]:
        total = total + product(back_of(g, j))
    for j in ring[::-1]:
        slab_copy(chips + j, back_of(partner, j), partner).wait_recv()
        total = total + product(back_of(partner, j))
    for copy in sends:
        copy.wait_send()
    parts = total[: 2 * owned_rows] + pltpu.roll(total[: 2 * owned_rows], LANES - comps, 1) + total[2 * owned_rows :]
    by_re, by_im = parts[:owned_rows], parts[owned_rows:]
    lane_own = iota((owned_rows, LANES), 1)
    solved = by_re + jnp.where(
        lane_own < rhs_count, -pltpu.roll(by_im, LANES - rhs_count, 1), pltpu.roll(by_im, rhs_count, 1)
    )

    back = lax.dot_general(
        row_map, solved, (((0,), (0,)), ((), ())), precision=HIGHEST, preferred_element_type=F32
    )
    ret_send[:, 0, :] = pack_slots(back, tiles)
    send_rows(ret_send, ret_got, 2)
    ret_got[pl.ds(t, 1)] = ret_send[pl.ds(t, 1)]
    wait_rows(ret_send, ret_got, 2)
    back = unpack_slots(ret_got[:, 0, :])
    back = jnp.concatenate([back, jnp.zeros((LANES - 3 * tiles, LANES), F32)], axis=0)
    values = back.T[:comps]
    placed = (values[:, None, :] * plane_map[None]).reshape(comps * plane_rows, LANES)
    extra = dot(placed, x_map, (1, 1)).reshape(2, rhs_count, plane_rows, LANES)
    drn[:, :, 0] = drn[:, :, 0] + extra[:, :, :height]
    drn[:, :, :, 0, :] = drn[:, :, :, 0, :] + extra[:, :, height:]

    pack_halo(drn, 1)
    d_halo = halo_copies(drn, 1)
    for copy in d_halo[::-1]:
        copy.start()
    for copy in d_halo:
        copy.wait()

    acc[...] = jnp.zeros_like(acc)

    def image_of(r, carry):
        re, im = operator(drn, 1, r)
        img[0, r] = re
        img[1, r] = im
        res_re, res_im = res[0, r], res[1, r]
        for i, value in enumerate(
            [re * res_re + im * res_im, re * res_im - im * res_re, re * re + im * im]
        ):
            acc[pl.ds(i * rhs_count + r, 1), :] = jnp.sum(jnp.sum(value, axis=0), axis=0, keepdims=True)
        return carry

    lax.fori_loop(0, rhs_count, image_of, 0)

    ones = jnp.ones((8, LANES), F32)
    sum_send[...] = dot(ones, acc[...], (1, 1))[:1]
    spread(sum_send, sum_got, 3)
    sum_got[t] = sum_send[...]
    wait_spread(sum_send, sum_got, 3)
    sum2_send[...] = jnp.sum(sum_got[...], axis=0)

    def sum_copy(j, row, peer):
        return remote(
            sum2_send, sum2_got.at[row], slab_send_sem.at[1, j], slab_recv_sem.at[1, j], peer, t
        )

    for j in range(1, slabs):
        sum_copy(j, g, lax.rem(g + j, slabs)).start()
    sum2_got[g] = sum2_send[...]
    for j in range(1, slabs):
        source = lax.rem(g + slabs - j, slabs)
        sum_copy(j, source, source).wait()
    totals = dot(sum2_got[:, 0, :], jnp.ones((slabs, LANES), F32), (0, 0))
    denom = totals[2 * rhs_count : 3 * rhs_count] + 1e-06
    alpha[0] = totals[:rhs_count] / denom
    alpha[1] = totals[rhs_count : 2 * rhs_count] / denom

    def update(r, carry):
        a_re = alpha[0, pl.ds(r, 1), :][None]
        a_im = alpha[1, pl.ds(r, 1), :][None]
        d_re, d_im = drn[0, r], drn[1, r]
        sol_ref[0, r] = x[0, r] + a_re * d_re - a_im * d_im
        sol_ref[1, r] = x[1, r] + a_re * d_im + a_im * d_re
        i_re, i_im = img[0, r], img[1, r]
        new_ref[0, r] = res[0, r] - a_re * i_re + a_im * i_im
        new_ref[1, r] = res[1, r] - a_re * i_im - a_im * i_re
        return carry

    lax.fori_loop(0, rhs_count, update, 0)


def local(x_start, rhs, wave_sq, damping, front, front_order, pair_count, sep_cell):
    slabs, tiles = lax.axis_size("gz"), lax.axis_size("xy")
    _, rhs_count, depth, height, width = x_start.shape
    field = pltpu.VMEM(x_start.shape, F32)
    any_space = pl.BlockSpec(memory_space=pl.ANY)
    vmem = pl.BlockSpec(memory_space=pltpu.VMEM)
    rows = pltpu.VMEM((tiles, 1, LANES), F32)
    dma = pltpu.SemaphoreType.DMA
    return pl.pallas_call(
        step,
        out_shape=(field, field),
        in_specs=[any_space] * 8,
        out_specs=(vmem, vmem),
        scratch_shapes=[
            field,
            field,
            pltpu.VMEM(wave_sq.shape, F32),
            pltpu.VMEM(wave_sq.shape, F32),
            pltpu.VMEM(front.shape, F32),
            pltpu.VMEM(front_order.shape, jnp.int32),
            pltpu.VMEM(pair_count.shape, jnp.int32),
            pltpu.VMEM(sep_cell.shape, jnp.int32),
            pltpu.VMEM((4 * front.shape[1], front.shape[2]), BF16),
            field,
            field,
            field,
            pltpu.VMEM((2,) + wave_sq.shape, F32),
            pltpu.VMEM((2, 2, 2, rhs_count, depth, width), F32),
            pltpu.VMEM((2, 4, 2, rhs_count, width), F32),
            pltpu.VMEM((2, 2, 2, rhs_count, height, width), F32),
            pltpu.VMEM((2, 2, 2, rhs_count, depth, width), F32),
            pltpu.VMEM((2, 4, 2, rhs_count, width), F32),
            rows,
            rows,
            pltpu.VMEM((4, LANES), F32),
            pltpu.VMEM((tiles, 4, LANES), F32),
            pltpu.VMEM((slabs * tiles // 4, 2 * rhs_count, LANES), F32),
            rows,
            rows,
            pltpu.VMEM((LANES, LANES), F32),
            pltpu.VMEM((1, LANES), F32),
            rows,
            pltpu.VMEM((1, LANES), F32),
            pltpu.VMEM((slabs, 1, LANES), F32),
            pltpu.VMEM((2, rhs_count, LANES), F32),
            dma((8,)),
            dma((2, 8)),
            dma((2, 8)),
            dma((4, tiles)),
            dma((4, tiles)),
            dma((2, slabs)),
            dma((2, slabs)),
        ],
        compiler_params=pltpu.CompilerParams(
            collective_id=0, has_side_effects=True, vmem_limit_bytes=60 * 1024 * 1024
        ),
    )(x_start, rhs, wave_sq, damping, front, front_order, pair_count, sep_cell)


def solution(mesh):
    in_specs = (
        P(None, None, "gz", "xy", None),
        P(None, None, "gz", "xy", None),
        P("gz", "xy", None),
        P("gz", "xy", None),
        P(None, ("gz", "xy"), None),
        P("gz", "xy", None),
        P("gz", None, None),
        P("gz", "xy", None),
    )
    out_specs = (P(None, None, "gz", "xy", None), P(None, None, "gz", "xy", None))
    return jax.shard_map(local, mesh=mesh, in_specs=in_specs, out_specs=out_specs, check_vma=False)
```

```python
import functools

import jax
import jax.numpy as jnp
from jax import lax
from jax.experimental import pallas as pl
from jax.experimental.pallas import tpu as pltpu
from jax.sharding import PartitionSpec as P

MESH = pl.DeviceIdType.MESH
HIGHEST = lax.Precision.HIGHEST
F32 = jnp.float32
BF16 = jnp.bfloat16
LANES = 128


def iota(shape, dim):
    return lax.broadcasted_iota(jnp.int32, shape, dim)


def dot(a, b, contract):
    return lax.dot_general(
        a, b, ((contract[:1], contract[1:]), ((), ())), precision=HIGHEST, preferred_element_type=F32
    )


def in_parts(value):
    high = value.astype(BF16)
    rest = value - high.astype(F32)
    middle = rest.astype(BF16)
    return high, middle, (rest - middle.astype(F32)).astype(BF16)


def pick_rows(value, one_hot, contract):
    rows = value.shape[0]
    out = lax.dot_general(
        jnp.concatenate(in_parts(value), axis=0), one_hot, (((1,), (contract,)), ((), ())), preferred_element_type=F32
    )
    return out[:rows] + out[rows : 2 * rows] + out[2 * rows :]


def x_sum(u):
    axis = u.ndim - 1
    lane = iota(u.shape, axis)
    left = jnp.where(lane > 0, pltpu.roll(u, 1, axis), 0.0)
    right = jnp.where(lane < LANES - 1, pltpu.roll(u, LANES - 1, axis), 0.0)
    return left + right


def side_rows(rows, edge_low, edge_high):
    depth = rows.shape[0]
    row_sum = x_sum(rows)
    m1 = 14.0 * rows + 3.0 * row_sum
    m2 = 3.0 * rows + row_sum
    edge = jnp.where(iota(rows.shape, 0) == 0, edge_low, edge_high)
    m2_edge = 3.0 * edge + x_sum(edge)
    z_pos = iota(rows.shape, 0)
    below = jnp.where(z_pos == 0, m2_edge, pltpu.roll(m2, 1, 0))
    above = jnp.where(z_pos == depth - 1, m2_edge, pltpu.roll(m2, depth - 1, 0))
    return m1 + below + above


def laplace(centre, z_low, z_high, y_low, y_high, edges):
    depth, height, _ = centre.shape
    padded = jnp.concatenate([z_low[None], centre, z_high[None]], axis=0)
    p = x_sum(padded)
    m1 = 14.0 * padded + 3.0 * p
    m2 = 3.0 * padded + p
    same = 128.0 * centre - 14.0 * p[1:-1] - (m1[:-2] + m1[2:])
    side = m1[1:-1] + m2[:-2] + m2[2:]
    low = side_rows(y_low, edges[0], edges[2])
    high = side_rows(y_high, edges[1], edges[3])
    y_pos = iota(centre.shape, 1)
    before = jnp.where(y_pos == 0, low[:, None, :], pltpu.roll(side, 1, 1))
    after = jnp.where(y_pos == height - 1, high[:, None, :], pltpu.roll(side, height - 1, 1))
    return (same - before - after) * (1.0 / 30.0)


def pack_slots(rows, tiles):
    lane = iota((tiles, LANES), 1)
    out = rows[:tiles]
    for k in range(1, 3):
        out = jnp.where(lane < 16 * k, out, pltpu.roll(rows[k * tiles : (k + 1) * tiles], 16 * k, 1))
    return out


def unpack_slots(rows):
    return jnp.concatenate([rows] + [pltpu.roll(rows, LANES - 16 * k, 1) for k in range(1, 3)], axis=0)


def step(
    x_hbm, rhs_hbm, wave_hbm, damp_hbm, front_hbm, order_hbm, count_hbm, cell_hbm,
    sol_ref, new_ref,
    x, rhs, wave, damp, front, order_ref, count_ref, cell_ref, split, res, drn, img, coef,
    y_send, e_send, z_got, y_got, e_got,
    slot_send, slot_got, own_send, own_got, vectors, ret_send, ret_got, fix_send, fix_got, cells_got, x_maps, acc, sum_send, sum_got, sum2_send, sum2_got, alpha,
    load_sem, cell_send_sem, cell_recv_sem, fix_send_sem, fix_recv_sem, halo_send_sem, halo_recv_sem, tile_send_sem, tile_recv_sem, slab_send_sem, slab_recv_sem,
):
    slabs, tiles = lax.axis_size("gz"), lax.axis_size("xy")
    g, t = lax.axis_index("gz"), lax.axis_index("xy")
    rhs_count, depth, height = x.shape[1], x.shape[2], x.shape[3]
    comps = 2 * rhs_count
    up_g, down_g = lax.rem(g + 1, slabs), lax.rem(g + slabs - 1, slabs)
    up_t, down_t = lax.rem(t + 1, tiles), lax.rem(t + tiles - 1, tiles)

    loads = [
        pltpu.make_async_copy(src, dst, load_sem.at[i])
        for i, (src, dst) in enumerate(
            [
                (x_hbm, x), (rhs_hbm, rhs), (wave_hbm, wave), (damp_hbm, damp), (front_hbm, front),
                (order_hbm, order_ref), (count_hbm, count_ref), (cell_hbm, cell_ref),
            ]
        )
    ]
    loads[0].start()
    barrier = pltpu.get_barrier_semaphore()

    def greet(gz, xy):
        pl.semaphore_signal(barrier, inc=1, device_id={"gz": gz, "xy": xy}, device_id_type=MESH)

    def greet_tile(j, carry):
        greet(g, lax.rem(t + j, tiles))
        return carry

    def greet_slab(j, carry):
        greet(lax.rem(g + j, slabs), t)
        return carry

    lax.fori_loop(1, tiles, greet_tile, 0)
    lax.fori_loop(1, slabs, greet_slab, 0)
    for gz in (up_g, down_g):
        for xy in (up_t, down_t):
            greet(gz, xy)
    for copy in loads[1:]:
        copy.start()

    def remote(src, dst, send_sem, recv_sem, gz, xy):
        return pltpu.make_async_remote_copy(
            src_ref=src, dst_ref=dst, send_sem=send_sem, recv_sem=recv_sem,
            device_id={"gz": gz, "xy": xy}, device_id_type=MESH,
        )

    def pack_halo(field, which):
        low, high = field[:, :, :, 0, :], field[:, :, :, height - 1, :]
        y_send[which, 0] = low
        y_send[which, 1] = high
        e_send[which, 0] = high[:, :, depth - 1, :]
        e_send[which, 1] = low[:, :, depth - 1, :]
        e_send[which, 2] = high[:, :, 0, :]
        e_send[which, 3] = low[:, :, 0, :]

    def halo_copies(field, which):
        todo = [
            (field.at[:, :, depth - 1], z_got.at[which, 0], up_g, t),
            (field.at[:, :, 0], z_got.at[which, 1], down_g, t),
            (y_send.at[which, 1], y_got.at[which, 0], g, up_t),
            (y_send.at[which, 0], y_got.at[which, 1], g, down_t),
            (e_send.at[which, 0], e_got.at[which, 0], up_g, up_t),
            (e_send.at[which, 1], e_got.at[which, 1], up_g, down_t),
            (e_send.at[which, 2], e_got.at[which, 2], down_g, up_t),
            (e_send.at[which, 3], e_got.at[which, 3], down_g, down_t),
        ]
        return [
            remote(src, dst, halo_send_sem.at[which, i], halo_recv_sem.at[which, i], gz, xy)
            for i, (src, dst, gz, xy) in enumerate(todo)
        ]

    has_down_g = (g > 0).astype(F32)
    has_up_g = (g < slabs - 1).astype(F32)
    has_down_t = (t > 0).astype(F32)
    has_up_t = (t < tiles - 1).astype(F32)

    def operator(field, which, r):
        parts = []
        for k in range(2):
            edges = [
                e_got[which, i, k, pl.ds(r, 1), :] * flag
                for i, flag in enumerate(
                    [has_down_g * has_down_t, has_down_g * has_up_t, has_up_g * has_down_t, has_up_g * has_up_t]
                )
            ]
            parts.append(
                laplace(
                    field[k, r],
                    z_got[which, 0, k, r] * has_down_g,
                    z_got[which, 1, k, r] * has_up_g,
                    y_got[which, 0, k, r] * has_down_t,
                    y_got[which, 1, k, r] * has_up_t,
                    edges,
                )
            )
        re, im = field[0, r], field[1, r]
        w, wd = wave[...], damp[...]
        return parts[0] - w * re + wd * im, parts[1] - w * im - wd * re

    def send_rows(send, got, bank):
        def start(j, carry):
            peer = lax.rem(t + j, tiles)
            remote(
                send.at[peer], got.at[t], tile_send_sem.at[bank, peer], tile_recv_sem.at[bank, t], g, peer
            ).start()
            return carry

        lax.fori_loop(1, tiles, start, 0)

    def wait_rows(send, got, bank):
        def wait(j, carry):
            peer = lax.rem(t + j, tiles)
            remote(
                send.at[peer], got.at[peer], tile_send_sem.at[bank, peer], tile_recv_sem.at[bank, peer], g, peer
            ).wait()
            return carry

        lax.fori_loop(1, tiles, wait, 0)

    def spread(send, got, bank):
        def start(j, carry):
            peer = lax.rem(t + j, tiles)
            remote(send, got.at[t], tile_send_sem.at[bank, peer], tile_recv_sem.at[bank, t], g, peer).start()
            return carry

        lax.fori_loop(1, tiles, start, 0)

    def wait_spread(send, got, bank):
        def wait(j, carry):
            peer = lax.rem(t + j, tiles)
            remote(
                send, got.at[peer], tile_send_sem.at[bank, peer], tile_recv_sem.at[bank, peer], g, peer
            ).wait()
            return carry

        lax.fori_loop(1, tiles, wait, 0)

    loads[0].wait()
    pack_halo(x, 0)
    x_halo = halo_copies(x, 0)
    around = [(dg, dt) for dg in (-1, 0, 1) for dt in (-1, 0, 1)]
    own = around.index((0, 0))
    cell_copies = [
        remote(
            cell_ref.at[0], cells_got.at[n], cell_send_sem.at[n], cell_recv_sem.at[n],
            lax.rem(g - dg + slabs, slabs), lax.rem(t - dt + tiles, tiles),
        )
        for n, (dg, dt) in enumerate(around)
        if n not in (0, own)
    ]
    loads[7].wait()
    for n in (0, own):
        cells_got[n] = cell_ref[0]
    pl.semaphore_wait(barrier, tiles - 1 + slabs - 1 + 4)
    for copy in x_halo[::-1] + cell_copies:
        copy.start()

    loads[2].wait()
    loads[3].wait()
    w = wave[...]
    wd = w * damp[...]
    damp[...] = wd
    diag_re = 128.0 / 30.0 - w
    diag_im = -wd
    modulus = diag_re * diag_re + diag_im * diag_im
    coef[0] = diag_re / modulus
    coef[1] = diag_im / modulus

    for copy in loads[5:7]:
        copy.wait()
    counts = count_ref[0, pl.ds(t, 1), :].astype(F32)
    spread_lane = iota((tiles, LANES), 1)
    spread_row = iota((tiles, LANES), 0)
    rank = spread_lane // tiles
    live = spread_lane < 3 * tiles
    take = jnp.where(live & (spread_row == spread_lane % tiles), 1.0, 0.0)
    earlier = jnp.where(live & (spread_row < spread_lane % tiles), 1.0, 0.0)
    counts8 = jnp.broadcast_to(counts, (8, tiles))
    count_at = dot(counts8, take, (1, 0))[:1]
    entry_at = dot(counts8, earlier, (1, 0))[:1] + rank[:1].astype(F32)
    entry_map = jnp.where((rank.astype(F32) < count_at) & (spread_row.astype(F32) == entry_at), 1.0, 0.0)
    order = order_ref[0, 0:1, :]
    order_map = jnp.where(iota((tiles, tiles), 0) == order, 1.0, 0.0)
    row_map = dot(order_map, entry_map, (1, 0))

    slots = cell_ref.shape[2]
    slot_row = iota((slots, LANES), 0)
    slot_lane = iota((slots, LANES), 1)
    slot_pick = jnp.where(
        (slot_lane < slots) & (slot_row == 3 * (slot_lane % tiles) + slot_lane // tiles), 1.0, 0.0
    )
    plane_rows = height + depth

    def places(cells):
        cell_at = (dot(cells.astype(F32), slot_pick, (1, 0)) + 0.5).astype(jnp.int32)
        return cell_at % LANES, (cell_at // LANES) % height, cell_at // (LANES * height)

    def x_map_of(cell_x):
        return jnp.where(iota((LANES, LANES), 0) == cell_x, 1.0, 0.0).astype(BF16)

    cell_x, cell_y, cell_z = [v[:1] for v in places(jnp.broadcast_to(cell_ref[0], (8, slots)))]
    x_map = x_map_of(cell_x)
    plane_row = jnp.where(cell_z == 0, cell_y, height + cell_z)
    plane_map = jnp.where(iota((plane_rows, LANES), 0) == plane_row, 1.0, 0.0)

    loads[4].wait()
    owned_rows = front.shape[1]
    chunk = 1024

    def split_front(i, carry):
        columns = pl.ds(pl.multiple_of(i * chunk, chunk), chunk)
        for k in range(2):
            value = front[k, :, columns]
            high = value.astype(BF16)
            split[k * owned_rows : (k + 1) * owned_rows, columns] = high
            split[(2 + k) * owned_rows : (3 + k) * owned_rows, columns] = (value - high.astype(F32)).astype(BF16)
        return carry

    lax.fori_loop(0, front.shape[2] // chunk, split_front, 0)

    loads[1].wait()
    for copy in x_halo:
        copy.wait()

    def residual_of(r, carry):
        re, im = operator(x, 0, r)
        re = rhs[0, r] - re
        im = rhs[1, r] - im
        res[0, r] = re
        res[1, r] = im
        drn[0, r] = re * coef[0] + im * coef[1]
        drn[1, r] = im * coef[0] - re * coef[1]
        return carry

    lax.fori_loop(0, rhs_count, residual_of, 0)

    planes = jnp.concatenate(
        [
            res[:, :, 0].reshape(comps, height, LANES),
            res[:, :, :, 0, :].reshape(comps, depth, LANES),
        ],
        axis=1,
    ).reshape(comps * plane_rows, LANES)
    hits = pick_rows(planes, x_map, 0).reshape(comps, plane_rows, LANES)
    values = jnp.sum(hits * plane_map[None], axis=1)
    values = jnp.concatenate([values, jnp.zeros((LANES - comps, LANES), F32)], axis=0)
    slot_send[:, 0, :] = pack_slots(values.T, tiles)
    send_rows(slot_send, slot_got, 0)
    slot_got[pl.ds(t, 1)] = slot_send[pl.ds(t, 1)]

    pack_halo(drn, 1)
    d_halo = halo_copies(drn, 1)
    for copy in d_halo[::-1]:
        copy.start()
    for copy in cell_copies:
        copy.wait()
    near_x, near_y, near_z = places(cells_got[:, 0, :])
    for n in range(len(around)):
        x_maps[n] = x_map_of(near_x[n : n + 1])

    wait_rows(slot_send, slot_got, 0)

    by_slot = unpack_slots(slot_got[:, 0, :])
    lane = iota((8, LANES), 1)
    rows4 = jnp.concatenate([row_map[:, : 3 * tiles]] * (LANES // owned_rows), axis=0)
    wide = pick_rows(by_slot.T[:comps], rows4.astype(BF16), 1)
    first, second = wide[:8], wide[8:16]
    block = jnp.where(
        lane < 32, first,
        jnp.where(lane < 64, pltpu.roll(first, 4, 0), jnp.where(lane < 96, second, pltpu.roll(second, 4, 0))),
    )
    own_send[...] = block[:4]
    spread(own_send, own_got, 1)
    own_got[t] = block[:4]
    wait_spread(own_send, own_got, 1)

    groups = tiles // 4
    got = own_got[...].reshape(groups, 4, 4, LANES)
    lane3 = iota((groups, 4, LANES), 2)
    for m in range(4):
        mine = None
        for b in range(4):
            shift = ((b - m) * 32) % LANES
            piece = got[:, b] if shift == 0 else pltpu.roll(got[:, b], shift, 2)
            mine = piece if mine is None else jnp.where(lane3 < 32 * b, mine, piece)
        vectors[pl.ds(g * groups, groups), 4 * m : 4 * m + 4, :] = mine

    partner = g + 1 - 2 * lax.rem(g, 2)
    chips = slabs // 2

    def slab_copy(j, source, peer):
        where = pl.ds(source * groups, groups)
        return remote(
            vectors.at[where], vectors.at[where], slab_send_sem.at[0, j], slab_recv_sem.at[0, j], peer, t
        )

    def back_of(base, j):
        return lax.rem(base + slabs - 2 * j, slabs)

    width = groups * LANES

    def product(source):
        vec = jnp.concatenate([vectors[source * groups + a] for a in range(groups)], axis=1)
        high = vec.astype(BF16)
        low = (vec - high.astype(F32)).astype(BF16)
        both = jnp.concatenate([high, low, jnp.zeros((LANES - 2 * comps, vec.shape[1]), BF16)], axis=0)
        columns = pl.ds(pl.multiple_of(source * width, width), width)
        return lax.dot_general(
            split[:, columns], both, (((1,), (1,)), ((), ())), preferred_element_type=F32
        )

    ring = sorted(range(1, chips), key=lambda j: -min(j, chips - j))
    sends = [slab_copy(j, g, lax.rem(g + 2 * j, slabs)) for j in ring] + [slab_copy(chips, g, partner)]
    for copy in sends:
        copy.start()
    total = product(g)
    for j in ring[::-1]:
        slab_copy(j, back_of(g, j), back_of(g, j)).wait_recv()
        onward = slab_copy(chips + j, back_of(g, j), partner)
        onward.start()
        sends.append(onward)
    slab_copy(chips, partner, partner).wait_recv()
    total = total + product(partner)
    for j in ring[::-1]:
        total = total + product(back_of(g, j))
    for j in ring[::-1]:
        slab_copy(chips + j, back_of(partner, j), partner).wait_recv()
        total = total + product(back_of(partner, j))
    for copy in sends:
        copy.wait_send()
    parts = total[: 2 * owned_rows] + pltpu.roll(total[: 2 * owned_rows], LANES - comps, 1) + total[2 * owned_rows :]
    by_re, by_im = parts[:owned_rows], parts[owned_rows:]
    lane_own = iota((owned_rows, LANES), 1)
    solved = by_re + jnp.where(
        lane_own < rhs_count, -pltpu.roll(by_im, LANES - rhs_count, 1), pltpu.roll(by_im, rhs_count, 1)
    )

    back = lax.dot_general(
        row_map.astype(BF16), jnp.concatenate(in_parts(solved), axis=1), (((0,), (0,)), ((), ())),
        preferred_element_type=F32,
    )
    packed = pack_slots(back[:, :LANES] + back[:, LANES : 2 * LANES] + back[:, 2 * LANES :], tiles)
    ret_send[1 : tiles + 1, 0, :] = packed
    ret_send[0] = packed[tiles - 1 :]
    ret_send[tiles + 1] = packed[:1]

    def ret_copy(peer, row):
        return remote(
            ret_send.at[pl.ds(peer, 3)], ret_got.at[row], tile_send_sem.at[2, peer], tile_recv_sem.at[2, row], g, peer
        )

    def start_ret(j, carry):
        ret_copy(lax.rem(t + j, tiles), t).start()
        return carry

    def wait_ret(j, carry):
        peer = lax.rem(t + j, tiles)
        ret_copy(peer, peer).wait()
        return carry

    lax.fori_loop(1, tiles, start_ret, 0)
    ret_got[t] = ret_send[pl.ds(t, 3)]
    for copy in d_halo:
        copy.wait()
    lax.fori_loop(1, tiles, wait_ret, 0)
    for i in range(3):
        back = unpack_slots(ret_got[:, i, 0, :])
        back = jnp.concatenate([back, jnp.zeros((LANES - 3 * tiles, LANES), F32)], axis=0)
        fix_send[i] = back.T[:comps]
    fix_copies = [
        remote(fix_send, fix_got.at[i], fix_send_sem.at[i], fix_recv_sem.at[i], gz, t)
        for i, gz in enumerate((up_g, down_g))
    ]
    for copy in fix_copies:
        copy.start()

    def place_rows(values, n, mask):
        rows = mask.shape[0]
        placed = (values[:, None, :] * mask[None]).reshape(comps * rows, LANES)
        return pick_rows(placed, x_maps[n], 1).reshape(2, rhs_count, rows, LANES)

    def place_row(values, n, z, y):
        mask = jnp.where((near_z[n : n + 1] == z) & (near_y[n : n + 1] == y), 1.0, 0.0)
        return pick_rows(values * mask, x_maps[n], 1).reshape(2, rhs_count, LANES)

    extra = place_rows(fix_send[1], own, plane_map)
    drn[:, :, 0] = drn[:, :, 0] + extra[:, :, :height]
    drn[:, :, :, 0, :] = drn[:, :, :, 0, :] + extra[:, :, height:]
    n = around.index((0, 1))
    face = jnp.where((near_y[n : n + 1] == 0) & (iota((depth, LANES), 0) == near_z[n : n + 1]), 1.0, 0.0)
    y_got[1, 1] = y_got[1, 1] + place_rows(fix_send[2], n, face)
    n = around.index((0, -1))
    y_got[1, 0, :, :, 0, :] = y_got[1, 0, :, :, 0, :] + place_row(fix_send[0], n, 0, height - 1)
    for copy in fix_copies:
        copy.wait()
    n = around.index((1, 0))
    face = jnp.where((near_z[n : n + 1] == 0) & (iota((height, LANES), 0) == near_y[n : n + 1]), 1.0, 0.0)
    z_got[1, 1] = z_got[1, 1] + place_rows(fix_got[1, 1], n, face)
    n = around.index((-1, 0))
    z_got[1, 0, :, :, 0, :] = z_got[1, 0, :, :, 0, :] + place_row(fix_got[0, 1], n, depth - 1, 0)
    e_got[1, 3] = e_got[1, 3] + place_row(fix_got[1, 2], around.index((1, 1)), 0, 0)
    e_got[1, 2] = e_got[1, 2] + place_row(fix_got[1, 0], around.index((1, -1)), 0, height - 1)
    e_got[1, 1] = e_got[1, 1] + place_row(fix_got[0, 2], around.index((-1, 1)), depth - 1, 0)

    acc[...] = jnp.zeros_like(acc)

    def image_of(r, carry):
        re, im = operator(drn, 1, r)
        img[0, r] = re
        img[1, r] = im
        res_re, res_im = res[0, r], res[1, r]
        for i, value in enumerate(
            [re * res_re + im * res_im, re * res_im - im * res_re, re * re + im * im]
        ):
            acc[pl.ds(i * rhs_count + r, 1), :] = jnp.sum(jnp.sum(value, axis=0), axis=0, keepdims=True)
        return carry

    lax.fori_loop(0, rhs_count, image_of, 0)

    ones = jnp.ones((8, LANES), F32)
    sum_send[...] = dot(ones, acc[...], (1, 1))[:1]
    spread(sum_send, sum_got, 3)
    sum_got[t] = sum_send[...]
    wait_spread(sum_send, sum_got, 3)
    sum2_send[...] = jnp.sum(sum_got[...], axis=0)

    def sum_copy(j, row, peer):
        return remote(
            sum2_send, sum2_got.at[row], slab_send_sem.at[1, j], slab_recv_sem.at[1, j], peer, t
        )

    for j in range(1, slabs):
        sum_copy(j, g, lax.rem(g + j, slabs)).start()
    sum2_got[g] = sum2_send[...]
    for j in range(1, slabs):
        source = lax.rem(g + slabs - j, slabs)
        sum_copy(j, source, source).wait()
    totals = dot(sum2_got[:, 0, :], jnp.ones((slabs, LANES), F32), (0, 0))
    denom = totals[2 * rhs_count : 3 * rhs_count] + 1e-06
    alpha[0] = totals[:rhs_count] / denom
    alpha[1] = totals[rhs_count : 2 * rhs_count] / denom

    def update(r, carry):
        a_re = alpha[0, pl.ds(r, 1), :][None]
        a_im = alpha[1, pl.ds(r, 1), :][None]
        d_re, d_im = drn[0, r], drn[1, r]
        sol_ref[0, r] = x[0, r] + a_re * d_re - a_im * d_im
        sol_ref[1, r] = x[1, r] + a_re * d_im + a_im * d_re
        i_re, i_im = img[0, r], img[1, r]
        new_ref[0, r] = res[0, r] - a_re * i_re + a_im * i_im
        new_ref[1, r] = res[1, r] - a_re * i_im - a_im * i_re
        return carry

    lax.fori_loop(0, rhs_count, update, 0)


def local(x_start, rhs, wave_sq, damping, front, front_order, pair_count, sep_cell):
    slabs, tiles = lax.axis_size("gz"), lax.axis_size("xy")
    _, rhs_count, depth, height, width = x_start.shape
    field = pltpu.VMEM(x_start.shape, F32)
    any_space = pl.BlockSpec(memory_space=pl.ANY)
    vmem = pl.BlockSpec(memory_space=pltpu.VMEM)
    rows = pltpu.VMEM((tiles, 1, LANES), F32)
    dma = pltpu.SemaphoreType.DMA
    return pl.pallas_call(
        step,
        out_shape=(field, field),
        in_specs=[any_space] * 8,
        out_specs=(vmem, vmem),
        scratch_shapes=[
            field,
            field,
            pltpu.VMEM(wave_sq.shape, F32),
            pltpu.VMEM(wave_sq.shape, F32),
            pltpu.VMEM(front.shape, F32),
            pltpu.VMEM(front_order.shape, jnp.int32),
            pltpu.VMEM(pair_count.shape, jnp.int32),
            pltpu.VMEM(sep_cell.shape, jnp.int32),
            pltpu.VMEM((4 * front.shape[1], front.shape[2]), BF16),
            field,
            field,
            field,
            pltpu.VMEM((2,) + wave_sq.shape, F32),
            pltpu.VMEM((2, 2, 2, rhs_count, depth, width), F32),
            pltpu.VMEM((2, 4, 2, rhs_count, width), F32),
            pltpu.VMEM((2, 2, 2, rhs_count, height, width), F32),
            pltpu.VMEM((2, 2, 2, rhs_count, depth, width), F32),
            pltpu.VMEM((2, 4, 2, rhs_count, width), F32),
            rows,
            rows,
            pltpu.VMEM((4, LANES), F32),
            pltpu.VMEM((tiles, 4, LANES), F32),
            pltpu.VMEM((slabs * tiles // 4, 2 * rhs_count, LANES), F32),
            pltpu.VMEM((tiles + 2, 1, LANES), F32),
            pltpu.VMEM((tiles, 3, 1, LANES), F32),
            pltpu.VMEM((3, 2 * rhs_count, LANES), F32),
            pltpu.VMEM((2, 3, 2 * rhs_count, LANES), F32),
            pltpu.VMEM((9, 1, sep_cell.shape[2]), jnp.int32),
            pltpu.VMEM((9, LANES, LANES), BF16),
            pltpu.VMEM((LANES, LANES), F32),
            pltpu.VMEM((1, LANES), F32),
            rows,
            pltpu.VMEM((1, LANES), F32),
            pltpu.VMEM((slabs, 1, LANES), F32),
            pltpu.VMEM((2, rhs_count, LANES), F32),
            dma((8,)),
            dma((9,)),
            dma((9,)),
            dma((2,)),
            dma((2,)),
            dma((2, 8)),
            dma((2, 8)),
            dma((4, tiles)),
            dma((4, tiles)),
            dma((2, slabs)),
            dma((2, slabs)),
        ],
        compiler_params=pltpu.CompilerParams(
            collective_id=0, has_side_effects=True, vmem_limit_bytes=60 * 1024 * 1024
        ),
    )(x_start, rhs, wave_sq, damping, front, front_order, pair_count, sep_cell)


def solution(mesh):
    in_specs = (
        P(None, None, "gz", "xy", None),
        P(None, None, "gz", "xy", None),
        P("gz", "xy", None),
        P("gz", "xy", None),
        P(None, ("gz", "xy"), None),
        P("gz", "xy", None),
        P("gz", None, None),
        P("gz", "xy", None),
    )
    out_specs = (P(None, None, "gz", "xy", None), P(None, None, "gz", "xy", None))
    return jax.shard_map(local, mesh=mesh, in_specs=in_specs, out_specs=out_specs, check_vma=False)
```

```python
import functools

import jax
import jax.numpy as jnp
from jax import lax
from jax.experimental import pallas as pl
from jax.experimental.pallas import tpu as pltpu
from jax.sharding import PartitionSpec as P

MESH = pl.DeviceIdType.MESH
HIGHEST = lax.Precision.HIGHEST
F32 = jnp.float32
BF16 = jnp.bfloat16
LANES = 128


def iota(shape, dim):
    return lax.broadcasted_iota(jnp.int32, shape, dim)


def dot(a, b, contract):
    return lax.dot_general(
        a, b, ((contract[:1], contract[1:]), ((), ())), precision=HIGHEST, preferred_element_type=F32
    )


def in_parts(value):
    high = value.astype(BF16)
    rest = value - high.astype(F32)
    middle = rest.astype(BF16)
    return high, middle, (rest - middle.astype(F32)).astype(BF16)


def pick_rows(value, one_hot, contract):
    rows = value.shape[0]
    out = lax.dot_general(
        jnp.concatenate(in_parts(value), axis=0), one_hot, (((1,), (contract,)), ((), ())), preferred_element_type=F32
    )
    return out[:rows] + out[rows : 2 * rows] + out[2 * rows :]


def x_sum(u):
    axis = u.ndim - 1
    lane = iota(u.shape, axis)
    left = jnp.where(lane > 0, pltpu.roll(u, 1, axis), 0.0)
    right = jnp.where(lane < LANES - 1, pltpu.roll(u, LANES - 1, axis), 0.0)
    return left + right


def side_rows(rows, edge_low, edge_high):
    depth = rows.shape[0]
    row_sum = x_sum(rows)
    m1 = 14.0 * rows + 3.0 * row_sum
    m2 = 3.0 * rows + row_sum
    edge = jnp.where(iota(rows.shape, 0) == 0, edge_low, edge_high)
    m2_edge = 3.0 * edge + x_sum(edge)
    z_pos = iota(rows.shape, 0)
    below = jnp.where(z_pos == 0, m2_edge, pltpu.roll(m2, 1, 0))
    above = jnp.where(z_pos == depth - 1, m2_edge, pltpu.roll(m2, depth - 1, 0))
    return m1 + below + above


def plane_term(plane, edge_low=None, edge_high=None):
    height = plane.shape[0]
    p = x_sum(plane)
    m2 = 3.0 * plane + p
    y_pos = iota(plane.shape, 0)
    m2_edge = 0.0
    if edge_low is not None:
        edge = jnp.where(y_pos == 0, edge_low, edge_high)
        m2_edge = 3.0 * edge + x_sum(edge)
    before = jnp.where(y_pos == 0, m2_edge, pltpu.roll(m2, 1, 0))
    after = jnp.where(y_pos == height - 1, m2_edge, pltpu.roll(m2, height - 1, 0))
    return 14.0 * plane + 3.0 * p + before + after


def laplace_inside(centre):
    depth, height, _ = centre.shape
    blank = jnp.zeros_like(centre[:1])

    def z_sum(u):
        return jnp.concatenate([blank, u[:-1]], axis=0) + jnp.concatenate([u[1:], blank], axis=0)

    p = x_sum(centre)
    m1 = 14.0 * centre + 3.0 * p
    m2 = 3.0 * centre + p
    same = 128.0 * centre - 14.0 * p - z_sum(m1)
    side = m1 + z_sum(m2)
    y_pos = iota(centre.shape, 1)
    before = jnp.where(y_pos == 0, 0.0, pltpu.roll(side, 1, 1))
    after = jnp.where(y_pos == height - 1, 0.0, pltpu.roll(side, height - 1, 1))
    return (same - before - after) * (1.0 / 30.0)


def laplace(centre, z_low, z_high, y_low, y_high, edges):
    depth, height, _ = centre.shape
    padded = jnp.concatenate([z_low[None], centre, z_high[None]], axis=0)
    p = x_sum(padded)
    m1 = 14.0 * padded + 3.0 * p
    m2 = 3.0 * padded + p
    same = 128.0 * centre - 14.0 * p[1:-1] - (m1[:-2] + m1[2:])
    side = m1[1:-1] + m2[:-2] + m2[2:]
    low = side_rows(y_low, edges[0], edges[2])
    high = side_rows(y_high, edges[1], edges[3])
    y_pos = iota(centre.shape, 1)
    before = jnp.where(y_pos == 0, low[:, None, :], pltpu.roll(side, 1, 1))
    after = jnp.where(y_pos == height - 1, high[:, None, :], pltpu.roll(side, height - 1, 1))
    return (same - before - after) * (1.0 / 30.0)


def pack_slots(rows, tiles):
    lane = iota((tiles, LANES), 1)
    out = rows[:tiles]
    for k in range(1, 3):
        out = jnp.where(lane < 16 * k, out, pltpu.roll(rows[k * tiles : (k + 1) * tiles], 16 * k, 1))
    return out


def unpack_slots(rows):
    return jnp.concatenate([rows] + [pltpu.roll(rows, LANES - 16 * k, 1) for k in range(1, 3)], axis=0)


def step(
    x_hbm, rhs_hbm, wave_hbm, damp_hbm, front_hbm, order_hbm, count_hbm, cell_hbm,
    x, drn, res, img, alpha,
    rhs, wave, damp, front, order_ref, count_ref, cell_ref, split, coef,
    y_send, e_send, z_got, y_got, e_got,
    slot_send, slot_got, own_send, own_got, vectors, ret_send, ret_got, fix_send, fix_got, cells_got, x_maps, z_fix, e_fix, acc, sum_send, sum_got, sum2_send, sum2_got,
    load_sem, cell_send_sem, cell_recv_sem, fix_send_sem, fix_recv_sem, halo_send_sem, halo_recv_sem, tile_send_sem, tile_recv_sem, slab_send_sem, slab_recv_sem,
):
    slabs, tiles = lax.axis_size("gz"), lax.axis_size("xy")
    g, t = lax.axis_index("gz"), lax.axis_index("xy")
    rhs_count, depth, height = x.shape[1], x.shape[2], x.shape[3]
    comps = 2 * rhs_count
    up_g, down_g = lax.rem(g + 1, slabs), lax.rem(g + slabs - 1, slabs)
    up_t, down_t = lax.rem(t + 1, tiles), lax.rem(t + tiles - 1, tiles)

    loads = [
        pltpu.make_async_copy(src, dst, load_sem.at[i])
        for i, (src, dst) in enumerate(
            [
                (x_hbm, x), (rhs_hbm, rhs), (wave_hbm, wave), (damp_hbm, damp), (front_hbm, front),
                (order_hbm, order_ref), (count_hbm, count_ref), (cell_hbm, cell_ref),
            ]
        )
    ]
    loads[0].start()
    barrier = pltpu.get_barrier_semaphore()

    def greet(gz, xy):
        pl.semaphore_signal(barrier, inc=1, device_id={"gz": gz, "xy": xy}, device_id_type=MESH)

    def greet_tile(j, carry):
        greet(g, lax.rem(t + j, tiles))
        return carry

    def greet_slab(j, carry):
        greet(lax.rem(g + j, slabs), t)
        return carry

    lax.fori_loop(1, tiles, greet_tile, 0)
    lax.fori_loop(1, slabs, greet_slab, 0)
    for gz in (up_g, down_g):
        for xy in (up_t, down_t):
            greet(gz, xy)
    for copy in loads[1:]:
        copy.start()

    def remote(src, dst, send_sem, recv_sem, gz, xy):
        return pltpu.make_async_remote_copy(
            src_ref=src, dst_ref=dst, send_sem=send_sem, recv_sem=recv_sem,
            device_id={"gz": gz, "xy": xy}, device_id_type=MESH,
        )

    def pack_halo(field, which):
        low, high = field[:, :, :, 0, :], field[:, :, :, height - 1, :]
        y_send[which, 0] = low
        y_send[which, 1] = high
        e_send[which, 0] = high[:, :, depth - 1, :]
        e_send[which, 1] = low[:, :, depth - 1, :]
        e_send[which, 2] = high[:, :, 0, :]
        e_send[which, 3] = low[:, :, 0, :]

    def halo_copies(field, which):
        todo = [
            (field.at[:, :, depth - 1], z_got.at[which, 0], up_g, t),
            (field.at[:, :, 0], z_got.at[which, 1], down_g, t),
            (y_send.at[which, 1], y_got.at[which, 0], g, up_t),
            (y_send.at[which, 0], y_got.at[which, 1], g, down_t),
            (e_send.at[which, 0], e_got.at[which, 0], up_g, up_t),
            (e_send.at[which, 1], e_got.at[which, 1], up_g, down_t),
            (e_send.at[which, 2], e_got.at[which, 2], down_g, up_t),
            (e_send.at[which, 3], e_got.at[which, 3], down_g, down_t),
        ]
        return [
            remote(src, dst, halo_send_sem.at[which, i], halo_recv_sem.at[which, i], gz, xy)
            for i, (src, dst, gz, xy) in enumerate(todo)
        ]

    has_down_g = (g > 0).astype(F32)
    has_up_g = (g < slabs - 1).astype(F32)
    has_down_t = (t > 0).astype(F32)
    has_up_t = (t < tiles - 1).astype(F32)

    def halo_of(which, k, r):
        flags = [has_down_g * has_down_t, has_down_g * has_up_t, has_up_g * has_down_t, has_up_g * has_up_t]
        edges = [e_got[which, i, k, pl.ds(r, 1), :] * flag for i, flag in enumerate(flags)]
        return (
            z_got[which, 0, k, r] * has_down_g,
            z_got[which, 1, k, r] * has_up_g,
            y_got[which, 0, k, r] * has_down_t,
            y_got[which, 1, k, r] * has_up_t,
            edges,
        )

    def diagonal(field, r, parts):
        re, im = field[0, r], field[1, r]
        w, wd = wave[...], damp[...]
        return parts[0] - w * re + wd * im, parts[1] - w * im - wd * re

    def send_rows(send, got, bank):
        def start(j, carry):
            peer = lax.rem(t + j, tiles)
            remote(
                send.at[peer], got.at[t], tile_send_sem.at[bank, peer], tile_recv_sem.at[bank, t], g, peer
            ).start()
            return carry

        lax.fori_loop(1, tiles, start, 0)

    def wait_rows(send, got, bank):
        def wait(j, carry):
            peer = lax.rem(t + j, tiles)
            remote(
                send.at[peer], got.at[peer], tile_send_sem.at[bank, peer], tile_recv_sem.at[bank, peer], g, peer
            ).wait()
            return carry

        lax.fori_loop(1, tiles, wait, 0)

    def spread(send, got, bank):
        def start(j, carry):
            peer = lax.rem(t + j, tiles)
            remote(send, got.at[t], tile_send_sem.at[bank, peer], tile_recv_sem.at[bank, t], g, peer).start()
            return carry

        lax.fori_loop(1, tiles, start, 0)

    def wait_spread(send, got, bank):
        def wait(j, carry):
            peer = lax.rem(t + j, tiles)
            remote(
                send, got.at[peer], tile_send_sem.at[bank, peer], tile_recv_sem.at[bank, peer], g, peer
            ).wait()
            return carry

        lax.fori_loop(1, tiles, wait, 0)

    loads[0].wait()
    pack_halo(x, 0)
    x_halo = halo_copies(x, 0)
    around = [(dg, dt) for dg in (-1, 0, 1) for dt in (-1, 0, 1)]
    own = around.index((0, 0))
    cell_copies = [
        remote(
            cell_ref.at[0], cells_got.at[n], cell_send_sem.at[n], cell_recv_sem.at[n],
            lax.rem(g - dg + slabs, slabs), lax.rem(t - dt + tiles, tiles),
        )
        for n, (dg, dt) in enumerate(around)
        if n not in (0, own)
    ]
    loads[7].wait()
    for n in (0, own):
        cells_got[n] = cell_ref[0]
    pl.semaphore_wait(barrier, tiles - 1 + slabs - 1 + 4)
    for copy in x_halo[::-1] + cell_copies:
        copy.start()

    loads[2].wait()
    loads[3].wait()
    w = wave[...]
    wd = w * damp[...]
    damp[...] = wd
    diag_re = 128.0 / 30.0 - w
    diag_im = -wd
    modulus = diag_re * diag_re + diag_im * diag_im
    coef[0] = diag_re / modulus
    coef[1] = diag_im / modulus

    for copy in loads[5:7]:
        copy.wait()
    counts = count_ref[0, pl.ds(t, 1), :].astype(F32)
    spread_lane = iota((tiles, LANES), 1)
    spread_row = iota((tiles, LANES), 0)
    rank = spread_lane // tiles
    live = spread_lane < 3 * tiles
    take = jnp.where(live & (spread_row == spread_lane % tiles), 1.0, 0.0)
    earlier = jnp.where(live & (spread_row < spread_lane % tiles), 1.0, 0.0)
    counts8 = jnp.broadcast_to(counts, (8, tiles))
    count_at = dot(counts8, take, (1, 0))[:1]
    entry_at = dot(counts8, earlier, (1, 0))[:1] + rank[:1].astype(F32)
    entry_map = jnp.where((rank.astype(F32) < count_at) & (spread_row.astype(F32) == entry_at), 1.0, 0.0)
    order = order_ref[0, 0:1, :]
    order_map = jnp.where(iota((tiles, tiles), 0) == order, 1.0, 0.0)
    row_map = dot(order_map, entry_map, (1, 0))

    slots = cell_ref.shape[2]
    slot_row = iota((slots, LANES), 0)
    slot_lane = iota((slots, LANES), 1)
    slot_pick = jnp.where(
        (slot_lane < slots) & (slot_row == 3 * (slot_lane % tiles) + slot_lane // tiles), 1.0, 0.0
    )
    plane_rows = height + depth

    def places(cells):
        cell_at = (dot(cells.astype(F32), slot_pick, (1, 0)) + 0.5).astype(jnp.int32)
        return cell_at % LANES, (cell_at // LANES) % height, cell_at // (LANES * height)

    def x_map_of(cell_x):
        return jnp.where(iota((LANES, LANES), 0) == cell_x, 1.0, 0.0).astype(BF16)

    cell_x, cell_y, cell_z = [v[:1] for v in places(jnp.broadcast_to(cell_ref[0], (8, slots)))]
    x_map = x_map_of(cell_x)
    plane_row = jnp.where(cell_z == 0, cell_y, height + cell_z)
    plane_map = jnp.where(iota((plane_rows, LANES), 0) == plane_row, 1.0, 0.0)

    loads[1].wait()

    def residual_inside(r, carry):
        re, im = diagonal(x, r, [laplace_inside(x[k, r]) for k in range(2)])
        res[0, r] = rhs[0, r] - re
        res[1, r] = rhs[1, r] - im
        return carry

    lax.fori_loop(0, rhs_count, residual_inside, 0)
    for copy in x_halo:
        copy.wait()

    def residual_edge(r, carry):
        for k in range(2):
            z_low, z_high, y_low, y_high, edges = halo_of(0, k, r)
            res[k, r, 0] = res[k, r, 0] + plane_term(z_low) * (1.0 / 30.0)
            res[k, r, depth - 1] = res[k, r, depth - 1] + plane_term(z_high) * (1.0 / 30.0)
            low = side_rows(y_low, edges[0], edges[2]) * (1.0 / 30.0)
            high = side_rows(y_high, edges[1], edges[3]) * (1.0 / 30.0)
            res[k, r, :, 0, :] = res[k, r, :, 0, :] + low
            res[k, r, :, height - 1, :] = res[k, r, :, height - 1, :] + high
        return carry

    lax.fori_loop(0, rhs_count, residual_edge, 0)

    planes = jnp.concatenate(
        [
            res[:, :, 0].reshape(comps, height, LANES),
            res[:, :, :, 0, :].reshape(comps, depth, LANES),
        ],
        axis=1,
    ).reshape(comps * plane_rows, LANES)
    hits = pick_rows(planes, x_map, 0).reshape(comps, plane_rows, LANES)
    values = jnp.sum(hits * plane_map[None], axis=1)
    values = jnp.concatenate([values, jnp.zeros((LANES - comps, LANES), F32)], axis=0)
    slot_send[:, 0, :] = pack_slots(values.T, tiles)
    send_rows(slot_send, slot_got, 0)
    slot_got[pl.ds(t, 1)] = slot_send[pl.ds(t, 1)]

    def scale(r, carry):
        re, im = res[0, r], res[1, r]
        drn[0, r] = re * coef[0] + im * coef[1]
        drn[1, r] = im * coef[0] - re * coef[1]
        return carry

    lax.fori_loop(0, rhs_count, scale, 0)

    pack_halo(drn, 1)
    d_halo = halo_copies(drn, 1)
    for copy in d_halo[::-1]:
        copy.start()
    for copy in cell_copies:
        copy.wait()
    near_x, near_y, near_z = places(cells_got[:, 0, :])
    for n in range(len(around)):
        x_maps[n] = x_map_of(near_x[n : n + 1])

    loads[4].wait()
    owned_rows = front.shape[1]
    chunk = 1024

    def split_front(i, carry):
        columns = pl.ds(pl.multiple_of(i * chunk, chunk), chunk)
        for k in range(2):
            value = front[k, :, columns]
            high = value.astype(BF16)
            split[k * owned_rows : (k + 1) * owned_rows, columns] = high
            split[(2 + k) * owned_rows : (3 + k) * owned_rows, columns] = (value - high.astype(F32)).astype(BF16)
        return carry

    lax.fori_loop(0, front.shape[2] // chunk, split_front, 0)

    wait_rows(slot_send, slot_got, 0)

    by_slot = unpack_slots(slot_got[:, 0, :])
    lane = iota((8, LANES), 1)
    rows4 = jnp.concatenate([row_map[:, : 3 * tiles]] * (LANES // owned_rows), axis=0)
    wide = pick_rows(by_slot.T[:comps], rows4.astype(BF16), 1)
    first, second = wide[:8], wide[8:16]
    block = jnp.where(
        lane < 32, first,
        jnp.where(lane < 64, pltpu.roll(first, 4, 0), jnp.where(lane < 96, second, pltpu.roll(second, 4, 0))),
    )
    own_send[...] = block[:4]
    spread(own_send, own_got, 1)
    own_got[t] = block[:4]
    wait_spread(own_send, own_got, 1)

    groups = tiles // 4
    got = own_got[...].reshape(groups, 4, 4, LANES)
    lane3 = iota((groups, 4, LANES), 2)
    for m in range(4):
        mine = None
        for b in range(4):
            shift = ((b - m) * 32) % LANES
            piece = got[:, b] if shift == 0 else pltpu.roll(got[:, b], shift, 2)
            mine = piece if mine is None else jnp.where(lane3 < 32 * b, mine, piece)
        vectors[pl.ds(g * groups, groups), 4 * m : 4 * m + 4, :] = mine

    partner = g + 1 - 2 * lax.rem(g, 2)
    chips = slabs // 2

    def slab_copy(j, source, peer):
        where = pl.ds(source * groups, groups)
        return remote(
            vectors.at[where], vectors.at[where], slab_send_sem.at[0, j], slab_recv_sem.at[0, j], peer, t
        )

    def back_of(base, j):
        return lax.rem(base + slabs - 2 * j, slabs)

    width = groups * LANES

    def product(source):
        vec = jnp.concatenate([vectors[source * groups + a] for a in range(groups)], axis=1)
        high = vec.astype(BF16)
        low = (vec - high.astype(F32)).astype(BF16)
        both = jnp.concatenate([high, low, jnp.zeros((LANES - 2 * comps, vec.shape[1]), BF16)], axis=0)
        columns = pl.ds(pl.multiple_of(source * width, width), width)
        return lax.dot_general(
            split[:, columns], both, (((1,), (1,)), ((), ())), preferred_element_type=F32
        )

    ring = sorted(range(1, chips), key=lambda j: -min(j, chips - j))
    sends = [slab_copy(j, g, lax.rem(g + 2 * j, slabs)) for j in ring] + [slab_copy(chips, g, partner)]
    for copy in sends:
        copy.start()
    total = product(g)
    for j in ring[::-1]:
        slab_copy(j, back_of(g, j), back_of(g, j)).wait_recv()
        onward = slab_copy(chips + j, back_of(g, j), partner)
        onward.start()
        sends.append(onward)
    slab_copy(chips, partner, partner).wait_recv()
    total = total + product(partner)
    for j in ring[::-1]:
        total = total + product(back_of(g, j))
    for j in ring[::-1]:
        slab_copy(chips + j, back_of(partner, j), partner).wait_recv()
        total = total + product(back_of(partner, j))
    for copy in sends:
        copy.wait_send()
    parts = total[: 2 * owned_rows] + pltpu.roll(total[: 2 * owned_rows], LANES - comps, 1) + total[2 * owned_rows :]
    by_re, by_im = parts[:owned_rows], parts[owned_rows:]
    lane_own = iota((owned_rows, LANES), 1)
    solved = by_re + jnp.where(
        lane_own < rhs_count, -pltpu.roll(by_im, LANES - rhs_count, 1), pltpu.roll(by_im, rhs_count, 1)
    )

    back = lax.dot_general(
        row_map.astype(BF16), jnp.concatenate(in_parts(solved), axis=1), (((0,), (0,)), ((), ())),
        preferred_element_type=F32,
    )
    packed = pack_slots(back[:, :LANES] + back[:, LANES : 2 * LANES] + back[:, 2 * LANES :], tiles)
    ret_send[1 : tiles + 1, 0, :] = packed
    ret_send[0] = packed[tiles - 1 :]
    ret_send[tiles + 1] = packed[:1]

    def ret_copy(peer, row):
        return remote(
            ret_send.at[pl.ds(peer, 3)], ret_got.at[row], tile_send_sem.at[2, peer], tile_recv_sem.at[2, row], g, peer
        )

    def start_ret(j, carry):
        ret_copy(lax.rem(t + j, tiles), t).start()
        return carry

    def wait_ret(j, carry):
        peer = lax.rem(t + j, tiles)
        ret_copy(peer, peer).wait()
        return carry

    lax.fori_loop(1, tiles, start_ret, 0)
    ret_got[t] = ret_send[pl.ds(t, 3)]
    for copy in d_halo:
        copy.wait()
    lax.fori_loop(1, tiles, wait_ret, 0)
    for i in range(3):
        back = unpack_slots(ret_got[:, i, 0, :])
        back = jnp.concatenate([back, jnp.zeros((LANES - 3 * tiles, LANES), F32)], axis=0)
        fix_send[i] = back.T[:comps]
    fix_copies = [
        remote(fix_send, fix_got.at[i], fix_send_sem.at[i], fix_recv_sem.at[i], gz, t)
        for i, gz in enumerate((up_g, down_g))
    ]
    for copy in fix_copies:
        copy.start()

    def place_rows(values, n, mask):
        rows = mask.shape[0]
        placed = (values[:, None, :] * mask[None]).reshape(comps * rows, LANES)
        return pick_rows(placed, x_maps[n], 1).reshape(2, rhs_count, rows, LANES)

    def place_row(values, n, z, y):
        mask = jnp.where((near_z[n : n + 1] == z) & (near_y[n : n + 1] == y), 1.0, 0.0)
        return pick_rows(values * mask, x_maps[n], 1).reshape(2, rhs_count, LANES)

    extra = place_rows(fix_send[1], own, plane_map)
    drn[:, :, 0] = drn[:, :, 0] + extra[:, :, :height]
    drn[:, :, :, 0, :] = drn[:, :, :, 0, :] + extra[:, :, height:]
    n = around.index((0, 1))
    face = jnp.where((near_y[n : n + 1] == 0) & (iota((depth, LANES), 0) == near_z[n : n + 1]), 1.0, 0.0)
    y_got[1, 1] = y_got[1, 1] + place_rows(fix_send[2], n, face)
    n = around.index((0, -1))
    y_got[1, 0, :, :, 0, :] = y_got[1, 0, :, :, 0, :] + place_row(fix_send[0], n, 0, height - 1)
    acc[...] = jnp.zeros_like(acc)

    def add_up(r, re, im, res_re, res_im):
        for i, value in enumerate(
            [re * res_re + im * res_im, re * res_im - im * res_re, re * re + im * im]
        ):
            row = pl.ds(i * rhs_count + r, 1)
            acc[row, :] = acc[row, :] + jnp.sum(jnp.sum(value, axis=0), axis=0, keepdims=True)

    def image_of(r, carry):
        re, im = diagonal(drn, r, [laplace(drn[k, r], *halo_of(1, k, r)) for k in range(2)])
        img[0, r] = re
        img[1, r] = im
        add_up(r, re[1:-1], im[1:-1], res[0, r, 1 : depth - 1], res[1, r, 1 : depth - 1])
        return carry

    lax.fori_loop(0, rhs_count, image_of, 0)

    for copy in fix_copies:
        copy.wait()
    n = around.index((1, 0))
    face = jnp.where((near_z[n : n + 1] == 0) & (iota((height, LANES), 0) == near_y[n : n + 1]), 1.0, 0.0)
    z_fix[1] = place_rows(fix_got[1, 1], n, face) * has_up_g
    z_fix[0] = jnp.zeros_like(z_fix[0])
    z_fix[0, :, :, 0, :] = place_row(fix_got[0, 1], around.index((-1, 0)), depth - 1, 0) * has_down_g
    e_fix[0] = place_row(fix_got[0, 2], around.index((-1, 1)), depth - 1, 0) * (has_down_g * has_up_t)
    e_fix[1] = place_row(fix_got[1, 0], around.index((1, -1)), 0, height - 1) * (has_up_g * has_down_t)
    e_fix[2] = place_row(fix_got[1, 2], around.index((1, 1)), 0, 0) * (has_up_g * has_up_t)

    def image_edge(r, carry):
        row = pl.ds(r, 1)
        ends = [[], []]
        for k in range(2):
            low = plane_term(z_fix[0, k, r], jnp.zeros((1, LANES), F32), e_fix[0, k, row, :])
            high = plane_term(z_fix[1, k, r], e_fix[1, k, row, :], e_fix[2, k, row, :])
            for side, (z, term) in enumerate(((0, low), (depth - 1, high))):
                value = img[k, r, z] - term * (1.0 / 30.0)
                img[k, r, z] = value
                ends[side].append(value)
        both = [jnp.stack([ends[0][k], ends[1][k]]) for k in range(2)]
        mine = [jnp.stack([res[k, r, 0], res[k, r, depth - 1]]) for k in range(2)]
        add_up(r, both[0], both[1], mine[0], mine[1])
        return carry

    lax.fori_loop(0, rhs_count, image_edge, 0)

    ones = jnp.ones((8, LANES), F32)
    sum_send[...] = dot(ones, acc[...], (1, 1))[:1]
    spread(sum_send, sum_got, 3)
    sum_got[t] = sum_send[...]
    wait_spread(sum_send, sum_got, 3)
    sum2_send[...] = jnp.sum(sum_got[...], axis=0)

    def sum_copy(j, row, peer):
        return remote(
            sum2_send, sum2_got.at[row], slab_send_sem.at[1, j], slab_recv_sem.at[1, j], peer, t
        )

    for j in range(1, slabs):
        sum_copy(j, g, lax.rem(g + j, slabs)).start()
    sum2_got[g] = sum2_send[...]
    for j in range(1, slabs):
        source = lax.rem(g + slabs - j, slabs)
        sum_copy(j, source, source).wait()
    totals = dot(sum2_got[:, 0, :], jnp.ones((slabs, LANES), F32), (0, 0))
    denom = totals[2 * rhs_count : 3 * rhs_count] + 1e-06
    alpha[0] = totals[:rhs_count] / denom
    alpha[1] = totals[rhs_count : 2 * rhs_count] / denom


def update(x_ref, drn_ref, res_ref, img_ref, alpha_ref, sol_ref, new_ref):
    r = pl.program_id(0)
    a_re = alpha_ref[0, pl.ds(r, 1), :][None]
    a_im = alpha_ref[1, pl.ds(r, 1), :][None]
    d_re, d_im = drn_ref[0, r], drn_ref[1, r]
    sol_ref[0, 0] = x_ref[0, r] + a_re * d_re - a_im * d_im
    sol_ref[1, 0] = x_ref[1, r] + a_re * d_im + a_im * d_re
    i_re, i_im = img_ref[0, r], img_ref[1, r]
    new_ref[0, 0] = res_ref[0, r] - a_re * i_re + a_im * i_im
    new_ref[1, 0] = res_ref[1, r] - a_re * i_im - a_im * i_re


def local(x_start, rhs, wave_sq, damping, front, front_order, pair_count, sep_cell):
    slabs, tiles = lax.axis_size("gz"), lax.axis_size("xy")
    _, rhs_count, depth, height, width = x_start.shape
    field = pltpu.VMEM(x_start.shape, F32)
    any_space = pl.BlockSpec(memory_space=pl.ANY)
    vmem = pl.BlockSpec(memory_space=pltpu.VMEM)
    rows = pltpu.VMEM((tiles, 1, LANES), F32)
    dma = pltpu.SemaphoreType.DMA
    kept = pl.pallas_call(
        step,
        out_shape=(field, field, field, field, pltpu.VMEM((2, rhs_count, LANES), F32)),
        in_specs=[any_space] * 8,
        out_specs=(vmem,) * 5,
        scratch_shapes=[
            field,
            pltpu.VMEM(wave_sq.shape, F32),
            pltpu.VMEM(wave_sq.shape, F32),
            pltpu.VMEM(front.shape, F32),
            pltpu.VMEM(front_order.shape, jnp.int32),
            pltpu.VMEM(pair_count.shape, jnp.int32),
            pltpu.VMEM(sep_cell.shape, jnp.int32),
            pltpu.VMEM((4 * front.shape[1], front.shape[2]), BF16),
            pltpu.VMEM((2,) + wave_sq.shape, F32),
            pltpu.VMEM((2, 2, 2, rhs_count, depth, width), F32),
            pltpu.VMEM((2, 4, 2, rhs_count, width), F32),
            pltpu.VMEM((2, 2, 2, rhs_count, height, width), F32),
            pltpu.VMEM((2, 2, 2, rhs_count, depth, width), F32),
            pltpu.VMEM((2, 4, 2, rhs_count, width), F32),
            rows,
            rows,
            pltpu.VMEM((4, LANES), F32),
            pltpu.VMEM((tiles, 4, LANES), F32),
            pltpu.VMEM((slabs * tiles // 4, 2 * rhs_count, LANES), F32),
            pltpu.VMEM((tiles + 2, 1, LANES), F32),
            pltpu.VMEM((tiles, 3, 1, LANES), F32),
            pltpu.VMEM((3, 2 * rhs_count, LANES), F32),
            pltpu.VMEM((2, 3, 2 * rhs_count, LANES), F32),
            pltpu.VMEM((9, 1, sep_cell.shape[2]), jnp.int32),
            pltpu.VMEM((9, LANES, LANES), BF16),
            pltpu.VMEM((2, 2, rhs_count, height, width), F32),
            pltpu.VMEM((3, 2, rhs_count, width), F32),
            pltpu.VMEM((LANES, LANES), F32),
            pltpu.VMEM((1, LANES), F32),
            rows,
            pltpu.VMEM((1, LANES), F32),
            pltpu.VMEM((slabs, 1, LANES), F32),
            dma((8,)),
            dma((9,)),
            dma((9,)),
            dma((2,)),
            dma((2,)),
            dma((2, 8)),
            dma((2, 8)),
            dma((4, tiles)),
            dma((4, tiles)),
            dma((2, slabs)),
            dma((2, slabs)),
        ],
        compiler_params=pltpu.CompilerParams(
            collective_id=0, has_side_effects=True, vmem_limit_bytes=58600000
        ),
    )(x_start, rhs, wave_sq, damping, front, front_order, pair_count, sep_cell)
    block = pl.BlockSpec((2, 1, depth, height, width), lambda r: (0, r, 0, 0, 0))
    result = jax.ShapeDtypeStruct(x_start.shape, F32)
    return tuple(
        pl.pallas_call(
            update,
            grid=(rhs_count,),
            out_shape=(result, result),
            in_specs=[vmem] * 5,
            out_specs=(block, block),
            compiler_params=pltpu.CompilerParams(vmem_limit_bytes=16 * 1024 * 1024),
        )(*kept)
    )


def solution(mesh):
    in_specs = (
        P(None, None, "gz", "xy", None),
        P(None, None, "gz", "xy", None),
        P("gz", "xy", None),
        P("gz", "xy", None),
        P(None, ("gz", "xy"), None),
        P("gz", "xy", None),
        P("gz", None, None),
        P("gz", "xy", None),
    )
    out_specs = (P(None, None, "gz", "xy", None), P(None, None, "gz", "xy", None))
    return jax.shard_map(local, mesh=mesh, in_specs=in_specs, out_specs=out_specs, check_vma=False)
```
